128 devices in a mesh: row: 4 (over y), col: 32 (over z, x, core).
Axes of the slice: x: 4, y: 4, z: 4, core: 2. Of those that a mesh axis runs over, the one named last changes fastest.
Arguments:
- hidden_in: bfloat16 [32768, 14336], P(('row', 'col')), may hold values from -6 to 6
- out_grad: bfloat16 [32768, 4096], P(('row', 'col')), may hold values from -6 to 6
- proj_in: bfloat16 [14336, 128], replicated, may hold values from -0.046875 to 0.046875
- proj_out: bfloat16 [4096, 128], replicated, may hold values from -0.09375 to 0.09375
- inverse_fisher: float32 [16384, 16384], P('row', 'col'), may hold values from -0.09375 to 0.09375
- queries: float32 [16384, 256], P('col'), may hold values from -6 to 6
- lengths: int32 [256], replicated, may hold values from 32 to 16640, as said below
- offsets: int32 [256], replicated, may hold values from 0 to 32767, as said below
Outputs:
- scores: float32 [256, 256], P(('row', 'col'))
The draws below stay inside these ranges and needn't reach their ends.
Inputs may be any that keep to these rules, and one draw needn't show every extreme that they name: `lengths`: every sample has 32 tokens or more, and one sample has exactly 32; one sample has exactly half of all slots plus 256, and that is the most. Samples follow one another in slot order, each after 0 to 3 unused slots; slots after the last sample are unused; offsets[s] + lengths[s] <= 32768.
All inputs are finite; a program needn't handle non-finite values.
Results may differ from the reference program's by a relative error of at most 0.0003.
Values sent between devices are 32-bit elements; how exact they have to be, the bound alone decides.
A program may use at most 128 MiB of HBM per device.

```python
import jax
import jax.numpy as jnp
from jax import lax

D = 4096
FF = 14336
RANK = 128
QUERIES = 256
LMIN = 32
TOK_DEV = 256
GRAD = 16384
TOKENS = 32768
SAMPLES = 256


def sample_layout(key):
    base = jax.random.fold_in(key, 7)
    key_weights = jax.random.fold_in(base, 1)
    key_pick = jax.random.fold_in(base, 2)
    key_gaps = jax.random.fold_in(base, 3)
    index_list = jnp.arange(SAMPLES, dtype=jnp.int32)
    longest = TOKENS // 2 + TOK_DEV
    weights = jax.random.randint(key_weights, (SAMPLES,), 1, 65).astype(jnp.int32)
    chosen = jax.random.randint(key_pick, (), 1, SAMPLES).astype(jnp.int32)
    weights = jnp.where((index_list == chosen) | (index_list == 0), 0, weights).astype(jnp.int32)
    gaps = jax.random.randint(key_gaps, (SAMPLES,), 0, 4).astype(jnp.int32)
    slack = TOKENS - longest - (SAMPLES - 1) * LMIN - jnp.sum(gaps)
    extra = weights * slack // jnp.sum(weights)
    lengths = jnp.where(index_list == 0, longest, LMIN + extra).astype(jnp.int32)
    sample_ends = jnp.cumsum(gaps + lengths).astype(jnp.int32)
    offsets = (sample_ends - lengths).astype(jnp.int32)
    return (lengths, offsets)


def draw_lengths(key, part):
    return sample_layout(key)[0]


def draw_offsets(key, part):
    return sample_layout(key)[1]


def with_spikes(result, stream_key, source, target, parts, factor):
    owner, partner = [(jnp.arange(result.shape[axis_at]) // (result.shape[axis_at] // parts)).reshape([-1 if axis == axis_at else 1 for axis in range(result.ndim)]) for axis_at in (source, target)]
    chosen = jax.random.permutation(stream_key, parts)[partner]
    strong = (owner == chosen) | (owner == (partner + parts // 2) % parts)
    return jnp.where(strong, factor * result, result)


def level_of(key, extent, cuts, least, largest):
    def one(dim, parts):
        draws = jax.random.uniform(jax.random.fold_in(jax.random.fold_in(key, 6), dim), (parts,), jnp.float32, least / len(cuts), largest / len(cuts))
        return jnp.repeat(jnp.exp(draws), extent[dim] // parts).reshape((-1,) + (1,) * (len(extent) - dim - 1))

    gain = one(*cuts[0])
    for cut in cuts[1:]:
        gain = gain * one(*cut)
    return gain


def centred(own_key, dims, scale, bound, pieces=(), held_as=jnp.bfloat16):
    drawn = jax.random.normal(own_key, dims, jnp.float32) * scale
    if len(pieces) > 0:
        drawn = level_of(own_key, dims, pieces, -0.22, 0.18) * drawn
    return jnp.clip(drawn, min=-bound, max=bound).astype(held_as)


def noise_with(rng, dims, deviation, most, shards, heavy, kind=jnp.bfloat16):
    values = deviation * jax.random.normal(rng, dims, jnp.float32)
    if shards:
        values = values * level_of(rng, dims, shards, -0.22, 0.18)
    return jnp.clip(with_spikes(values, jax.random.fold_in(rng, 3), *heavy), -most, most).astype(kind)


def setup_inputs(seed: int = 0) -> dict:
    splits = jax.random.split(jax.random.key(seed), 9)
    hidden_in = centred(splits[0], (TOKENS, FF), 1.0, 6.0, ((0, 128),))
    out_grad = centred(splits[1], (TOKENS, D), 1.0, 6.0, ((0, 128),))
    proj_in = centred(splits[2], (FF, RANK), FF ** -0.5, 0.046875)
    proj_out = centred(splits[3], (D, RANK), D ** -0.5, 0.09375)
    inverse_fisher = noise_with(splits[4], (GRAD, GRAD), GRAD ** -0.5, 0.09375, ((0, 4), (1, 32)), (1, 0, 32, 2.75), jnp.float32)
    queries = centred(splits[5], (GRAD, QUERIES), 1.0, 6.0, ((0, 32),), jnp.float32)
    lengths = draw_lengths(jax.random.fold_in(splits[8], 71), 0)
    offsets = draw_offsets(jax.random.fold_in(splits[8], 71), 0)
    return dict(hidden_in=hidden_in, out_grad=out_grad, proj_in=proj_in, proj_out=proj_out, inverse_fisher=inverse_fisher, queries=queries, lengths=lengths, offsets=offsets)


score_scale = 0.0625


def reference(hidden_in, out_grad, proj_in, proj_out, inverse_fisher, queries, lengths, offsets):
    proj_tokens = jnp.dot(hidden_in, proj_in, preferred_element_type=jnp.float32)
    proj_grads = jnp.dot(out_grad, proj_out, preferred_element_type=jnp.float32)
    sample_ends = offsets + lengths
    token_block = TOK_DEV
    block_count = TOKENS // token_block

    def scan_block(running, block_id):
        begin_row = (block_id * token_block).astype(jnp.int32)
        tokens_here = lax.dynamic_slice_in_dim(proj_tokens, begin_row, token_block, 0)
        grads_here = lax.dynamic_slice_in_dim(proj_grads, begin_row, token_block, 0)
        positions = begin_row + jnp.arange(token_block, dtype=jnp.int32)
        sample_id = jnp.sum((offsets[None, :] <= positions[:, None]).astype(jnp.int32), axis=1) - 1
        safe_id = jnp.clip(sample_id, 0, SAMPLES - 1).astype(jnp.int32)
        is_live = (sample_id >= 0) & (positions < sample_ends[safe_id])
        outer_terms = (grads_here[:, :, None] * tokens_here[:, None, :]).reshape(token_block, GRAD)
        outer_terms = outer_terms * is_live.astype(jnp.float32)[:, None]
        return running + jax.ops.segment_sum(outer_terms, safe_id, SAMPLES), None

    sample_grads, unused = lax.scan(scan_block, jnp.zeros((SAMPLES, GRAD), jnp.float32), jnp.arange(block_count, dtype=jnp.int32))
    precond = jnp.dot(inverse_fisher, queries, precision=lax.Precision.HIGHEST, preferred_element_type=jnp.float32)
    raw_scores = jnp.dot(sample_grads, precond, precision=lax.Precision.HIGHEST, preferred_element_type=jnp.float32)
    return score_scale * raw_scores / lengths.astype(jnp.float32)[:, None]
```

```python
import functools

import jax
import jax.numpy as jnp
from jax import lax
from jax.experimental import pallas as pl
from jax.experimental.pallas import tpu as pltpu
from jax.sharding import Mesh
from jax.sharding import PartitionSpec as P

AXES = ("row", "col_0", "col_1", "col_2")
WIN = 17
PITCH = 24
KCH = 2048
score_scale = 0.0625
f32 = jnp.float32
bf16 = jnp.bfloat16


def split(v):
    hi = v.astype(bf16)
    lo = (v - hi.astype(f32)).astype(bf16)
    return hi, lo


def dot(a, b):
    return jnp.dot(a, b, preferred_element_type=f32)


def kernel(
    f_ref, q_ref, h_ref, pi_ref, g_ref, po_ref, off_ref, len_ref, lens_ref,
    out_ref,
    fv, qv, hv, piv, gv, pov, q3,
    ua, ub, ca, cb,
    fa1, fb1, na1, nb1, fa2, fb2, na2, nb2,
    pt, pg, pgt, gsend, grecv, oneh, sbuf, srecv, sown, spart,
    fsem, qsem, hsem, gsem,
    csend, crecv, r_send, r_recv,
    psend, precv, gssem, grsem, sssem, srsem, xsend, xrecv,
):
    y = lax.axis_index("row")
    z = lax.axis_index("col_0")
    x = lax.axis_index("col_1")
    k = lax.axis_index("col_2")
    chip = y * 16 + z * 4 + x

    def remote(src, dst, ss, rs, dev):
        return pltpu.make_async_remote_copy(
            src_ref=src, dst_ref=dst, send_sem=ss, recv_sem=rs,
            device_id=dev, device_id_type=pl.DeviceIdType.MESH,
        )

    partner = (y, z, x, lax.rem(k + 1, 2))
    xp = (y, z, lax.rem(x + 1, 4), k)
    xm = (y, z, lax.rem(x + 3, 4), k)
    zp = (y, lax.rem(z + 1, 4), x, k)
    zm = (y, lax.rem(z + 3, 4), x, k)

    grecv[...] = jnp.zeros_like(grecv)

    barrier = pltpu.get_barrier_semaphore()

    @pl.loop(1, 128)
    def _(o):
        pl.semaphore_signal(
            barrier, inc=1,
            device_id=(
                lax.rem(y + o // 32, 4),
                lax.rem(z + (o // 8) % 4, 4),
                lax.rem(x + (o // 2) % 4, 4),
                lax.rem(k + o % 2, 2),
            ),
            device_id_type=pl.DeviceIdType.MESH,
        )

    qcopy = pltpu.make_async_copy(q_ref, qv, qsem.at[0])
    qcopy.start()

    def fcopy(g, dz):
        dk = 1 - g // 4
        dx = (6 - g % 4) % 4
        a = lax.rem(k + dk, 2) * 16 + lax.rem(x + dx, 4) * 4 + lax.rem(z + dz, 4)
        rows = pl.ds(pl.multiple_of(a * 128, 128), 128)
        return pltpu.make_async_copy(f_ref.at[rows], fv.at[g, dz], fsem.at[g, dz])

    @pl.loop(0, 32)
    def _(i):
        fcopy(i // 4, i % 4).start()

    def hcopies(c):
        cols = pl.ds(pl.multiple_of(c * KCH, KCH), KCH)
        return (
            pltpu.make_async_copy(h_ref.at[:, cols], hv.at[c], hsem.at[0, c]),
            pltpu.make_async_copy(pi_ref.at[cols], piv.at[c], hsem.at[1, c]),
        )

    def gcopies(c):
        cols = pl.ds(pl.multiple_of(c * KCH, KCH), KCH)
        return (
            pltpu.make_async_copy(g_ref.at[:, cols], gv.at[c], gsem.at[0, c]),
            pltpu.make_async_copy(po_ref.at[cols], pov.at[c], gsem.at[1, c]),
        )

    @pl.loop(0, 2)
    def _(c):
        for cp in gcopies(c):
            cp.start()

    @pl.loop(0, 7)
    def _(c):
        for cp in hcopies(c):
            cp.start()

    qcopy.wait()
    qh, ql = split(qv[...])
    q3[0:512] = qh
    q3[512:1024] = ql
    q3[1024:1536] = qh

    @pl.loop(0, 8)
    def _(g):
        for dz in range(4):
            fcopy(g, dz).wait()
        dk = 1 - g // 4
        dx = (6 - g % 4) % 4
        hi, lo = split(fv[g].reshape(512, 512))
        u = dot(jnp.concatenate([hi, hi, lo], axis=1), q3[...]).reshape(4, 128, 256)
        ua[dk, dx] = u[:, 0:64]
        for dz in range(4):
            ub[dk, dz, dx] = u[dz, 64:128]

    pl.semaphore_wait(barrier, 127)

    order = (2, 1, 3, 0)
    swaps = {}
    for n, q in enumerate(order):
        for c, (u, r) in enumerate(((ua, ca), (ub, cb))):
            cp = remote(u.at[1, q], r.at[q], csend.at[c, q], crecv.at[c, q], partner)
            cp.start()
            swaps[c, q] = cp

    done = list(swaps.values())

    def merge(c, q):
        u, r = ((ua, ca), (ub, cb))[c]
        swaps[c, q].wait_recv()
        u[0, q] = u[0, q] + r[q]

    class Ring:
        def __init__(self, p, half, far, near, ids, plus, minus):
            self.p, self.half, self.far, self.near = p, half, far, near
            self.ids, self.plus, self.minus = ids, plus, minus
            self.recv = {}

        def piece(self, q, h):
            return self.p.at[q, pl.ds(h * self.half, self.half)]

        def go(self, name, n, src, dst, dev):
            cp = remote(src, dst, r_send.at[self.ids, n], r_recv.at[self.ids, n], dev)
            cp.start()
            self.recv[name] = cp
            done.append(cp)

        def send_far(self):
            self.go("f0", 0, self.piece(2, 0), self.far.at[0], self.plus)
            self.go("f1", 1, self.piece(2, 1), self.far.at[1], self.minus)

        def part(self, i, h):
            return self.near.at[i, pl.ds(h * self.half, self.half)]

        def send_plus_early(self):
            self.go("p1", 2, self.piece(1, 1), self.part(0, 1), self.plus)

        def send_minus_early(self):
            self.go("m0", 3, self.piece(3, 0), self.part(1, 0), self.minus)

        def relay(self):
            self.recv["f0"].wait_recv()
            s = self.piece(1, 0)
            s[...] = s[...] + self.far[0]
            self.go("p0", 4, s, self.part(0, 0), self.plus)
            self.recv["f1"].wait_recv()
            s = self.piece(3, 1)
            s[...] = s[...] + self.far[1]
            self.go("m1", 5, s, self.part(1, 1), self.minus)

        def finish(self):
            for name in ("p1", "m0", "p0", "m1"):
                self.recv[name].wait_recv()
            self.p[0] = self.p[0] + self.near[0] + self.near[1]

    ring_a = Ring(ua.at[0], 2, fa1, na1, 0, xp, xm)
    ring_b = Ring(ub.at[0], 2, fb1, nb1, 1, zp, zm)
    ring_a2 = Ring(ua.at[0, 0], 32, fa2, na2, 2, zp, zm)
    ring_b2 = Ring(ub.at[0, 0], 32, fb2, nb2, 3, xp, xm)

    merge(0, 2)
    ring_a.send_far()
    merge(1, 2)
    ring_b.send_far()
    merge(0, 1)
    ring_a.send_plus_early()
    merge(1, 1)
    ring_b.send_plus_early()
    merge(0, 3)
    ring_a.send_minus_early()
    merge(1, 3)
    ring_b.send_minus_early()
    merge(0, 0)
    merge(1, 0)

    mine = pl.ds(pl.multiple_of(k * 256, 256), 256)
    pg[mine] = jnp.zeros((256, 128), f32)
    pt[mine] = jnp.zeros((256, 128), f32)

    @pl.loop(0, 2)
    def _(c):
        for cp in gcopies(c):
            cp.wait()
        pg[mine] = pg[mine] + dot(gv[c], pov[c])

    @pl.loop(0, 7)
    def _(c):
        for cp in hcopies(c):
            cp.wait()
        pt[mine] = pt[mine] + dot(hv[c], piv[c])

    give_g = remote(pg.at[mine], pg.at[mine], psend.at[0], precv.at[0], partner)
    give_t = remote(pt.at[mine], pt.at[mine], psend.at[1], precv.at[1], partner)
    give_g.start()
    give_t.start()
    done.extend((give_g, give_t))

    ring_a.relay()
    ring_b.relay()

    off_row = off_ref[...].astype(f32)
    end_row = off_row + len_ref[...].astype(f32)
    off_col = jnp.transpose(jnp.broadcast_to(off_row, (8, 256)))[:, 0:1]
    end_col = jnp.transpose(jnp.broadcast_to(end_row, (8, 256)))[:, 0:1]
    slot0 = (chip * 512).astype(f32)
    slots = lax.broadcasted_iota(jnp.int32, (1, 512), 1).astype(f32) + slot0
    begun = jnp.sum((off_col <= slots).astype(f32), axis=0, keepdims=True)
    ended = jnp.sum((end_col <= slots).astype(f32), axis=0, keepdims=True)
    passed = jnp.sum((end_col <= slot0).astype(f32), axis=0, keepdims=True)
    window = jnp.where(begun == ended + 1.0, begun - 1.0 - passed, -1.0)
    member = (
        lax.broadcasted_iota(jnp.int32, (PITCH, 512), 0).astype(f32) == window
    ).astype(f32)

    give_g.wait_recv()
    give_t.wait_recv()
    pgt[...] = jnp.transpose(pg[...]).reshape(8, 16, 512)
    th, tl = split(pt[...])
    t3 = jnp.concatenate([th, tl, th], axis=0)
    for yy in range(4):
        lines = pgt[yy * 2 + k]
        spread = (lines[:, None, :] * member[None, :, :]).reshape(16 * PITCH, 512)
        hi, lo = split(spread)
        grads = dot(jnp.concatenate([hi, hi, lo], axis=1), t3)
        gsend[yy * 16 : yy * 16 + 16] = grads.reshape(16, PITCH, 128)

    def peer(o):
        return (
            lax.rem(y + o // 16, 4),
            lax.rem(z + o % 4, 4),
            lax.rem(x + (o // 4) % 4, 4),
        )

    @pl.loop(1, 64)
    def _(o):
        py, pz, px = peer(o)
        remote(
            gsend.at[py * 16 + px * 4 + pz, pl.ds(0, WIN)],
            grecv.at[chip, pl.ds(0, WIN)],
            gssem.at[0], grsem.at[0], (py, pz, px, k),
        ).start()

    grecv[chip] = gsend[y * 16 + x * 4 + z]

    cols = lax.broadcasted_iota(jnp.int32, (1, 64 * PITCH), 1)
    col_chip = (cols * 2731) >> 16
    col_win = cols - col_chip * PITCH
    col_slot = (col_chip * 512).astype(f32)
    before = jnp.sum((end_col <= col_slot).astype(f32), axis=0, keepdims=True)
    target = jnp.where(col_win < WIN, before + col_win.astype(f32), -1.0)
    line = lax.broadcasted_iota(jnp.int32, (512, 1), 0)
    sample = (line >> 3) * 4 + ((line >> 2) & 1) * 2 + (line & 1)
    oneh[...] = (sample.astype(f32) == target).astype(f32).astype(bf16)

    ring_a.finish()
    ring_a2.send_far()
    ring_a2.send_plus_early()
    ring_a2.send_minus_early()
    ring_b.finish()
    ring_b2.send_far()
    ring_b2.send_plus_early()
    ring_b2.send_minus_early()
    ring_a2.relay()
    ring_b2.relay()
    ring_a2.finish()
    ring_b2.finish()

    uh, ul = split(jnp.concatenate([ua[0, 0, 0], ub[0, 0, 0]], axis=0))
    u3 = jnp.concatenate([uh, ul, uh], axis=0)

    pltpu.make_async_copy(
        grecv.at[pl.ds(0, 63), pl.ds(0, WIN)], grecv.at[pl.ds(0, 63), pl.ds(0, WIN)], grsem.at[0]
    ).wait()
    gh, gl = split(grecv[...].reshape(64 * PITCH, 128))
    dense = dot(oneh[...], gh) + dot(oneh[...], gl)
    dh, dl = split(dense)
    both = dot(jnp.concatenate([dh, dh, dl], axis=1), u3)
    upper = ((line >> 1) & 1) == 0
    sbuf[...] = jnp.where(upper, both[:, 0:128], both[:, 128:256]).reshape(64, 8, 128)

    @pl.loop(1, 64)
    def _(o):
        py, pz, px = peer(o)
        remote(
            sbuf.at[py * 16 + pz * 4 + px], srecv.at[chip],
            sssem.at[0], srsem.at[0], (py, pz, px, k),
        ).start()

    srecv[chip] = sbuf[chip]
    pltpu.make_async_copy(
        srecv.at[pl.ds(0, 63)], srecv.at[pl.ds(0, 63)], srsem.at[0]
    ).wait()
    sown[...] = jnp.sum(srecv[...], axis=0)
    last = remote(sown, spart, xsend.at[0], xrecv.at[0], partner)
    last.start()
    last.wait_recv()
    tile = sown[...] + spart[...]
    tile = jnp.where(k == 0, tile[0:4], tile[4:8]) * score_scale
    d = chip * 2 + k
    for s in range(2):
        n = lens_ref[2 * d + s].astype(f32)
        for j in range(2):
            out_ref[s : s + 1, j * 128 : j * 128 + 128] = tile[j * 2 + s : j * 2 + s + 1] / n

    last.wait_send()
    for cp in done:
        cp.wait_send()
    pltpu.make_async_copy(
        gsend.at[pl.ds(0, 63), pl.ds(0, WIN)], gsend.at[pl.ds(0, 63), pl.ds(0, WIN)], gssem.at[0]
    ).wait()
    pltpu.make_async_copy(sbuf.at[pl.ds(0, 63)], sbuf.at[pl.ds(0, 63)], sssem.at[0]).wait()


def body(hidden_in, out_grad, proj_in, proj_out, inverse_fisher, queries, lengths, offsets):
    vmem = pltpu.VMEM
    dma = pltpu.SemaphoreType.DMA
    anys = pl.BlockSpec(memory_space=pl.ANY)
    invm = pl.BlockSpec(memory_space=pltpu.VMEM)
    return pl.pallas_call(
        kernel,
        out_shape=jax.ShapeDtypeStruct((2, 256), f32),
        in_specs=[anys] * 6 + [invm] * 2 + [pl.BlockSpec(memory_space=pltpu.SMEM)],
        out_specs=invm,
        scratch_shapes=[
            vmem((8, 4, 128, 512), f32), vmem((512, 256), f32),
            vmem((7, 256, KCH), bf16), vmem((7, KCH, 128), bf16),
            vmem((2, 256, KCH), bf16), vmem((2, KCH, 128), bf16),
            vmem((1536, 256), bf16),
            vmem((2, 4, 4, 64, 256), f32), vmem((2, 4, 4, 64, 256), f32),
            vmem((4, 4, 64, 256), f32), vmem((4, 4, 64, 256), f32),
            vmem((2, 2, 64, 256), f32), vmem((2, 2, 64, 256), f32),
            vmem((2, 4, 64, 256), f32), vmem((2, 4, 64, 256), f32),
            vmem((2, 32, 256), f32), vmem((2, 32, 256), f32),
            vmem((2, 64, 256), f32), vmem((2, 64, 256), f32),
            vmem((512, 128), f32), vmem((512, 128), f32), vmem((8, 16, 512), f32),
            vmem((64, PITCH, 128), f32), vmem((64, PITCH, 128), f32),
            vmem((512, 64 * PITCH), bf16),
            vmem((64, 8, 128), f32), vmem((64, 8, 128), f32),
            vmem((8, 128), f32), vmem((8, 128), f32),
            dma((8, 4)), dma((1,)), dma((2, 7)), dma((2, 2)),
            dma((2, 4)), dma((2, 4)), dma((4, 6)), dma((4, 6)),
            dma((2,)), dma((2,)), dma((1,)), dma((1,)), dma((1,)), dma((1,)),
            dma((1,)), dma((1,)),
        ],
        compiler_params=pltpu.CompilerParams(
            collective_id=0, has_side_effects=True, vmem_limit_bytes=60 * 1024 * 1024
        ),
    )(
        inverse_fisher, queries, hidden_in, proj_in, out_grad, proj_out,
        offsets.reshape(1, 256), lengths.reshape(1, 256), lengths,
    )


def solution(mesh):
    whole = Mesh(mesh.devices.reshape(4, 4, 4, 2), AXES)
    col = AXES[1:]
    return jax.shard_map(
        body,
        mesh=whole,
        in_specs=(
            P(AXES, None), P(AXES, None), P(), P(), P("row", col), P(col, None), P(), P(),
        ),
        out_specs=P(AXES, None),
        check_vma=False,
    )
```

```python
import jax
import jax.numpy as jnp
from jax import lax
from jax.experimental import pallas as pl
from jax.experimental.pallas import tpu as pltpu
from jax.sharding import Mesh
from jax.sharding import PartitionSpec as P

AXES = ("row", "col_0", "col_1", "col_2")
WIN = 17
PITCH = 24
KCH = 2048
GROUPS = (
    ((2, 0), (2, 1), (2, 2), (2, 3)),
    ((1, 2), (3, 2), (0, 2), (1, 1)),
    ((1, 3), (1, 0), (3, 1), (0, 1)),
    ((3, 3), (3, 0), (0, 3), (0, 0)),
)
PEERS = sorted(
    ((i // 16, i // 4 % 4, i % 4) for i in range(1, 64)),
    key=lambda o: -sum(min(v, 4 - v) for v in o),
)
PLANE = ((2, 2), (2, 1), (1, 2), (2, 3), (3, 2), (1, 1), (1, 3), (3, 1), (3, 3),
         (0, 2), (2, 0), (0, 1), (1, 0), (0, 3), (3, 0), (0, 0))
TURNS = (2, 1, 3, 0)
score_scale = 0.0625
f32 = jnp.float32
bf16 = jnp.bfloat16


def split(v):
    hi = v.astype(bf16)
    lo = (v - hi.astype(f32)).astype(bf16)
    return hi, lo


def dot(a, b):
    return jnp.dot(a, b, preferred_element_type=f32)


def kernel(
    f_ref, q_ref, h_ref, pi_ref, g_ref, po_ref, off_ref, len_ref, lens_ref,
    out_ref,
    fv, qv, hv, piv, gv, pov, q3, fs,
    uu, cc, ua, ub,
    fa1, fb1, na1, nb1, fa2, fb2, na2, nb2,
    pt, pg, pgt, gsend, grecv, oneh, sbuf, srecv, sown, spart,
    fsem, qsem, hsem, gsem,
    csend, crecv, r_send, r_recv,
    plane_sem, all_sem, psend, precv, gssem, grsem, sssem, srsem, xsend, xrecv,
):
    y = lax.axis_index("row")
    z = lax.axis_index("col_0")
    x = lax.axis_index("col_1")
    k = lax.axis_index("col_2")
    chip = y * 16 + z * 4 + x

    def remote(src, dst, ss, rs, dev):
        return pltpu.make_async_remote_copy(
            src_ref=src, dst_ref=dst, send_sem=ss, recv_sem=rs,
            device_id=dev, device_id_type=pl.DeviceIdType.MESH,
        )

    partner = (y, z, x, lax.rem(k + 1, 2))
    xp = (y, z, lax.rem(x + 1, 4), k)
    xm = (y, z, lax.rem(x + 3, 4), k)
    zp = (y, lax.rem(z + 1, 4), x, k)
    zm = (y, lax.rem(z + 3, 4), x, k)

    xs = [x] + [lax.rem(x + i, 4) for i in (1, 2, 3)]
    zs = [z] + [lax.rem(z + i, 4) for i in (1, 2, 3)]
    ys = [y] + [lax.rem(y + i, 4) for i in (1, 2, 3)]
    ks = [k, lax.rem(k + 1, 2)]

    qcopy = pltpu.make_async_copy(q_ref, qv, qsem.at[0])
    qcopy.start()
    fcopies = {}
    for n, group in enumerate(GROUPS):
        for dk in (1, 0):
            for i, (dx, dz) in enumerate(group):
                a = ks[dk] * 16 + xs[dx] * 4 + zs[dz]
                rows = pl.ds(pl.multiple_of(a * 128, 128), 128)
                fcopies[n, dk, i] = pltpu.make_async_copy(
                    f_ref.at[rows], fv.at[n * 2 + dk, i], fsem.at[n * 2 + dk, i]
                )
    for i in range(4):
        fcopies[0, 1, i].start()

    grecv[...] = jnp.zeros_like(grecv)

    barrier = pltpu.get_barrier_semaphore()

    def greet(sem, dev):
        pl.semaphore_signal(sem, inc=1, device_id=dev, device_id_type=pl.DeviceIdType.MESH)

    greet(barrier, partner)
    for i in (1, 3, 2):
        greet(barrier, (y, z, xs[i], k))
        greet(barrier, (y, zs[i], x, k))
        greet(barrier, (ys[i], z, x, k))

    def hcopies(c):
        cols = pl.ds(c * KCH, KCH)
        return (
            pltpu.make_async_copy(h_ref.at[:, cols], hv.at[c], hsem.at[0, c]),
            pltpu.make_async_copy(pi_ref.at[cols], piv.at[c], hsem.at[1, c]),
        )

    def gcopies(c):
        cols = pl.ds(c * KCH, KCH)
        return (
            pltpu.make_async_copy(g_ref.at[:, cols], gv.at[c], gsem.at[0, c]),
            pltpu.make_async_copy(po_ref.at[cols], pov.at[c], gsem.at[1, c]),
        )

    qcopy.wait()
    for key, cp in fcopies.items():
        if key[:2] != (0, 1):
            cp.start()
    for c in range(2):
        for cp in gcopies(c):
            cp.start()
    for c in range(7):
        for cp in hcopies(c):
            cp.start()
    qh, ql = split(qv[...])
    q3[0:512] = qh
    q3[512:1024] = ql
    q3[1024:1536] = qh

    def prepare(n, dk):
        for i in range(4):
            fcopies[n, dk, i].wait()
        hi, lo = split(fv[n * 2 + dk].reshape(512, 512))
        fs[dk, 0] = hi
        fs[dk, 1] = lo

    def compute(n, dk):
        for i in range(2):
            hi, lo = (fs[dk, j, i * 256 : i * 256 + 256] for j in range(2))
            v = dot(jnp.concatenate([hi, hi, lo], axis=1), q3[...])
            uu[dk, n, i * 2 : i * 2 + 2] = v.reshape(2, 128, 256)

    done = []
    swaps = {}

    def swap(n):
        swaps[n] = remote(uu.at[1, n], cc.at[n], csend.at[n], crecv.at[n], partner)
        swaps[n].start()
        done.append(swaps[n])

    def merge(n):
        swaps[n].wait_recv()
        for i, (dx, dz) in enumerate(GROUPS[n]):
            v = uu[0, n, i] + cc[n, i]
            ua[dx, dz] = v[0:64]
            ub[dz, dx] = v[64:128]

    class Ring:
        def __init__(self, p, half, far, near, ids, plus, minus):
            self.p, self.half, self.far, self.near = p, half, far, near
            self.ids, self.plus, self.minus = ids, plus, minus
            self.recv = {}

        def piece(self, q, h):
            return self.p.at[q, pl.ds(h * self.half, self.half)]

        def go(self, name, n, src, dst, dev):
            cp = remote(src, dst, r_send.at[self.ids, n], r_recv.at[self.ids, n], dev)
            cp.start()
            self.recv[name] = cp
            done.append(cp)

        def send_far(self):
            self.go("f0", 0, self.piece(2, 0), self.far.at[0], self.plus)
            self.go("f1", 1, self.piece(2, 1), self.far.at[1], self.minus)

        def part(self, i, h):
            return self.near.at[i, pl.ds(h * self.half, self.half)]

        def send_plus_early(self):
            self.go("p1", 2, self.piece(1, 1), self.part(0, 1), self.plus)

        def send_minus_early(self):
            self.go("m0", 3, self.piece(3, 0), self.part(1, 0), self.minus)

        def relay(self):
            self.recv["f0"].wait_recv()
            s = self.piece(1, 0)
            s[...] = s[...] + self.far[0]
            self.go("p0", 4, s, self.part(0, 0), self.plus)
            self.recv["f1"].wait_recv()
            s = self.piece(3, 1)
            s[...] = s[...] + self.far[1]
            self.go("m1", 5, s, self.part(1, 1), self.minus)

        def finish(self):
            for name in ("p1", "m0", "p0", "m1"):
                self.recv[name].wait_recv()
            self.p[0] = self.p[0] + self.near[0] + self.near[1]

    ring_a = Ring(ua, 2, fa1, na1, 0, xp, xm)
    ring_b = Ring(ub, 2, fb1, nb1, 1, zp, zm)
    ring_a2 = Ring(ua.at[0], 32, fa2, na2, 2, zp, zm)
    ring_b2 = Ring(ub.at[0], 32, fb2, nb2, 3, xp, xm)

    prepare(0, 1)
    prepare(0, 0)
    compute(0, 1)
    pl.semaphore_wait(barrier, 10)
    for i in (1, 3, 2):
        greet(plane_sem, (y, zs[i], x, k))
    swap(0)
    prepare(1, 1)
    compute(0, 0)
    prepare(1, 0)
    compute(1, 1)
    swap(1)
    merge(0)
    ring_a.send_far()
    prepare(2, 1)
    compute(1, 0)
    prepare(2, 0)
    compute(2, 1)
    swap(2)
    merge(1)
    ring_b.send_far()
    prepare(3, 1)
    compute(2, 0)
    prepare(3, 0)
    compute(3, 1)
    swap(3)
    merge(2)
    ring_a.send_plus_early()
    ring_b.send_plus_early()
    compute(3, 0)
    pl.semaphore_wait(plane_sem, 3)
    for i in (1, 3, 2):
        greet(all_sem, (ys[i], z, x, k))
    merge(3)
    ring_a.send_minus_early()
    ring_b.send_minus_early()

    mine = pl.ds(pl.multiple_of(k * 256, 256), 256)

    def proj(store, copies, a, b, cs):
        for c in cs:
            for cp in copies(c):
                cp.wait()
            v = dot(a[c], b[c])
            store[mine] = v if c == 0 else store[mine] + v

    proj(pg, gcopies, gv, pov, range(2))
    proj(pt, hcopies, hv, piv, range(1))
    ring_a.relay()
    proj(pt, hcopies, hv, piv, range(1, 4))
    ring_b.relay()
    proj(pt, hcopies, hv, piv, range(4, 7))

    give_g = remote(pg.at[mine], pg.at[mine], psend.at[0], precv.at[0], partner)
    give_t = remote(pt.at[mine], pt.at[mine], psend.at[1], precv.at[1], partner)
    give_g.start()
    give_t.start()
    done.extend((give_g, give_t))

    off_row = off_ref[...].astype(f32)
    end_row = off_row + len_ref[...].astype(f32)
    off_col = jnp.transpose(jnp.broadcast_to(off_row, (8, 256)))[:, 0:1]
    end_col = jnp.transpose(jnp.broadcast_to(end_row, (8, 256)))[:, 0:1]
    slot0 = (chip * 512).astype(f32)
    slots = lax.broadcasted_iota(jnp.int32, (1, 512), 1).astype(f32) + slot0
    begun = jnp.sum((off_col <= slots).astype(f32), axis=0, keepdims=True)
    ended = jnp.sum((end_col <= slots).astype(f32), axis=0, keepdims=True)
    passed = jnp.sum((end_col <= slot0).astype(f32), axis=0, keepdims=True)
    window = jnp.where(begun == ended + 1.0, begun - 1.0 - passed, -1.0)
    member = (
        lax.broadcasted_iota(jnp.int32, (PITCH, 512), 0).astype(f32) == window
    ).astype(f32)

    give_g.wait_recv()
    give_t.wait_recv()
    pgt[...] = jnp.transpose(pg[...]).reshape(8, 16, 512)
    th, tl = split(pt[...])
    t3 = jnp.concatenate([th, tl, th], axis=0)
    for half in range(2):
        lines = jnp.concatenate([pgt[half * 4 + k], pgt[half * 4 + 2 + k]], axis=0)
        spread = (lines[:, None, :] * member[None, :, :]).reshape(32 * PITCH, 512)
        hi, lo = split(spread)
        rows = jnp.concatenate([hi, hi, lo], axis=1)
        grads = jnp.concatenate([dot(rows[i : i + 256], t3) for i in (0, 256, 512)], axis=0)
        gsend[half * 32 : half * 32 + 32] = grads.reshape(32, PITCH, 128)

    pl.semaphore_wait(all_sem, 3)

    def spread_grads(p):
        oy = TURNS[p]
        for oz, ox in PLANE:
            if (oy, oz, ox) != (0, 0, 0):
                remote(
                    gsend.at[ys[oy] * 16 + xs[ox] * 4 + zs[oz], pl.ds(0, WIN)],
                    grecv.at[p * 16 + oz * 4 + ox, pl.ds(0, WIN)],
                    gssem.at[0], grsem.at[p], (ys[oy], zs[oz], xs[ox], k),
                ).start()

    spread_grads(0)
    grecv[48] = gsend[y * 16 + x * 4 + z]

    cols = lax.broadcasted_iota(jnp.int32, (1, 64 * PITCH), 1)
    place = (cols * 2731) >> 16
    col_win = cols - place * PITCH
    turn = place >> 4
    from_y = y - jnp.where(turn == 0, 2, jnp.where(turn == 1, 1, jnp.where(turn == 2, 3, 0)))
    from_z = z - ((place >> 2) & 3)
    from_x = x - (place & 3)
    col_chip = (from_y & 3) * 16 + (from_z & 3) * 4 + (from_x & 3)
    col_slot = (col_chip * 512).astype(f32)
    before = jnp.sum((end_col <= col_slot).astype(f32), axis=0, keepdims=True)
    target = jnp.where(col_win < WIN, before + col_win.astype(f32), -1.0)
    line = lax.broadcasted_iota(jnp.int32, (512, 1), 0)
    sample = (line >> 3) * 4 + ((line >> 2) & 1) * 2 + (line & 1)
    oneh[...] = (sample.astype(f32) == target).astype(f32).astype(bf16)

    def gather_grads(first, count):
        for p in range(first // 16, (first + count) // 16):
            n = 15 if p == 3 else 16
            slots = grecv.at[pl.ds(p * 16, n), pl.ds(0, WIN)]
            pltpu.make_async_copy(slots, slots, grsem.at[p]).wait()
        part = pl.ds(first * PITCH, count * PITCH)
        gh, gl = split(grecv[first : first + count].reshape(count * PITCH, 128))
        gg = jnp.concatenate([gh, gl], axis=0)
        picks = (oneh[0:256, part], oneh[256:512, part])
        return [dot(jnp.concatenate([m, m], axis=1), gg) for m in picks]

    ring_a.finish()
    ring_a2.send_far()
    ring_a2.send_plus_early()
    ring_a2.send_minus_early()
    ring_b.finish()
    ring_b2.send_far()
    ring_b2.send_plus_early()
    ring_b2.send_minus_early()
    spread_grads(1)
    spread_grads(2)
    ring_a2.relay()
    ring_b2.relay()
    spread_grads(3)
    ring_a2.finish()
    ring_b2.finish()
    dense_a = gather_grads(0, 32)

    uh, ul = split(jnp.concatenate([ua[0, 0], ub[0, 0]], axis=0))
    u3 = jnp.concatenate([uh, ul, uh], axis=0)

    dense_b = gather_grads(32, 32)
    upper = ((line[0:256] >> 1) & 1) == 0
    for i in range(2):
        dh, dl = split(dense_a[i] + dense_b[i])
        both = dot(jnp.concatenate([dh, dh, dl], axis=1), u3)
        tiles = jnp.where(upper, both[:, 0:128], both[:, 128:256])
        sbuf[i * 32 : i * 32 + 32] = tiles.reshape(32, 8, 128)

    for oy, oz, ox in PEERS:
        remote(
            sbuf.at[ys[oy] * 16 + zs[oz] * 4 + xs[ox]], srecv.at[chip],
            sssem.at[0], srsem.at[0], (ys[oy], zs[oz], xs[ox], k),
        ).start()

    srecv[chip] = sbuf[chip]
    pltpu.make_async_copy(
        srecv.at[pl.ds(0, 63)], srecv.at[pl.ds(0, 63)], srsem.at[0]
    ).wait()
    sown[...] = jnp.sum(srecv[...], axis=0)
    last = remote(sown, spart, xsend.at[0], xrecv.at[0], partner)
    last.start()
    last.wait_recv()
    tile = sown[...] + spart[...]
    tile = jnp.where(k == 0, tile[0:4], tile[4:8]) * score_scale
    d = chip * 2 + k
    for s in range(2):
        n = lens_ref[2 * d + s].astype(f32)
        for j in range(2):
            out_ref[s : s + 1, j * 128 : j * 128 + 128] = tile[j * 2 + s : j * 2 + s + 1] / n

    last.wait_send()
    for cp in done:
        cp.wait_send()
    pltpu.make_async_copy(
        gsend.at[pl.ds(0, 63), pl.ds(0, WIN)], gsend.at[pl.ds(0, 63), pl.ds(0, WIN)], gssem.at[0]
    ).wait()
    pltpu.make_async_copy(sbuf.at[pl.ds(0, 63)], sbuf.at[pl.ds(0, 63)], sssem.at[0]).wait()


def body(hidden_in, out_grad, proj_in, proj_out, inverse_fisher, queries, lengths, offsets):
    vmem = pltpu.VMEM
    dma = pltpu.SemaphoreType.DMA
    anys = pl.BlockSpec(memory_space=pl.ANY)
    invm = pl.BlockSpec(memory_space=pltpu.VMEM)
    return pl.pallas_call(
        kernel,
        out_shape=jax.ShapeDtypeStruct((2, 256), f32),
        in_specs=[anys] * 6 + [invm] * 2 + [pl.BlockSpec(memory_space=pltpu.SMEM)],
        out_specs=invm,
        scratch_shapes=[
            vmem((8, 4, 128, 512), f32), vmem((512, 256), f32),
            vmem((7, 256, KCH), bf16), vmem((7, KCH, 128), bf16),
            vmem((2, 256, KCH), bf16), vmem((2, KCH, 128), bf16),
            vmem((1536, 256), bf16), vmem((2, 2, 512, 512), bf16),
            vmem((2, 4, 4, 128, 256), f32), vmem((4, 4, 128, 256), f32),
            vmem((4, 4, 64, 256), f32), vmem((4, 4, 64, 256), f32),
            vmem((2, 2, 64, 256), f32), vmem((2, 2, 64, 256), f32),
            vmem((2, 4, 64, 256), f32), vmem((2, 4, 64, 256), f32),
            vmem((2, 32, 256), f32), vmem((2, 32, 256), f32),
            vmem((2, 64, 256), f32), vmem((2, 64, 256), f32),
            vmem((512, 128), f32), vmem((512, 128), f32), vmem((8, 16, 512), f32),
            vmem((64, PITCH, 128), f32), vmem((64, PITCH, 128), f32),
            vmem((512, 64 * PITCH), bf16),
            vmem((64, 8, 128), f32), vmem((64, 8, 128), f32),
            vmem((8, 128), f32), vmem((8, 128), f32),
            dma((8, 4)), dma((1,)), dma((2, 7)), dma((2, 2)),
            dma((4,)), dma((4,)), dma((4, 6)), dma((4, 6)),
            pltpu.SemaphoreType.REGULAR, pltpu.SemaphoreType.REGULAR,
            dma((2,)), dma((2,)), dma((1,)), dma((4,)), dma((1,)), dma((1,)),
            dma((1,)), dma((1,)),
        ],
        compiler_params=pltpu.CompilerParams(
            collective_id=0, has_side_effects=True, vmem_limit_bytes=60 * 1024 * 1024
        ),
    )(
        inverse_fisher, queries, hidden_in, proj_in, out_grad, proj_out,
        offsets.reshape(1, 256), lengths.reshape(1, 256), lengths,
    )


def solution(mesh):
    whole = Mesh(mesh.devices.reshape(4, 4, 4, 2), AXES)
    col = AXES[1:]
    return jax.shard_map(
        body,
        mesh=whole,
        in_specs=(
            P(AXES, None), P(AXES, None), P(), P(), P("row", col), P(col, None), P(), P(),
        ),
        out_specs=P(AXES, None),
        check_vma=False,
    )
```

```python
import jax
import jax.numpy as jnp
from jax import lax
from jax.experimental import pallas as pl
from jax.experimental.pallas import tpu as pltpu
from jax.sharding import Mesh
from jax.sharding import PartitionSpec as P

AXES = ("row", "col_0", "col_1", "col_2")
WIN = 17
PITCH = 24
KCH = 2048
GROUPS = (
    ((2, 0), (2, 1), (2, 2), (2, 3)),
    ((1, 2), (3, 2), (0, 2), (1, 3)),
    ((3, 0), (3, 1), (0, 3), (1, 1)),
    ((1, 0), (3, 3), (0, 1), (0, 0)),
)
PEERS = sorted(
    ((i // 16, i // 4 % 4, i % 4) for i in range(1, 64)),
    key=lambda o: -sum(min(v, 4 - v) for v in o),
)
PLANE = ((2, 2), (2, 1), (1, 2), (2, 3), (3, 2), (1, 1), (1, 3), (3, 1), (3, 3),
         (0, 2), (2, 0), (0, 1), (1, 0), (0, 3), (3, 0), (0, 0))
TURNS = (2, 1, 3, 0)
score_scale = 0.0625
f32 = jnp.float32
bf16 = jnp.bfloat16


def split(v):
    hi = v.astype(bf16)
    lo = (v - hi.astype(f32)).astype(bf16)
    return hi, lo


def dot(a, b):
    return jnp.dot(a, b, preferred_element_type=f32)


def kernel(
    f_ref, q_ref, h_ref, pi_ref, g_ref, po_ref, off_ref, len_ref, lens_ref,
    out_ref,
    fv, qv, hv, piv, gv, pov, q3,
    uu, cc, ua, ub,
    fa1, fb1, na1, nb1, fa2, fb2, na2, nb2,
    pt, pg, pgt, gsend, grecv, oneh, sbuf, srecv, other,
    fsem, qsem, hsem, gsem,
    csend, crecv, r_send, r_recv,
    plane_sem, all_sem, psend, precv, gssem, grsem, sssem, srsem, xsend,
):
    y = lax.axis_index("row")
    z = lax.axis_index("col_0")
    x = lax.axis_index("col_1")
    k = lax.axis_index("col_2")
    chip = y * 16 + z * 4 + x

    def remote(src, dst, ss, rs, dev):
        return pltpu.make_async_remote_copy(
            src_ref=src, dst_ref=dst, send_sem=ss, recv_sem=rs,
            device_id=dev, device_id_type=pl.DeviceIdType.MESH,
        )

    partner = (y, z, x, lax.rem(k + 1, 2))
    xp = (y, z, lax.rem(x + 1, 4), k)
    xm = (y, z, lax.rem(x + 3, 4), k)
    zp = (y, lax.rem(z + 1, 4), x, k)
    zm = (y, lax.rem(z + 3, 4), x, k)

    xs = [x] + [lax.rem(x + i, 4) for i in (1, 2, 3)]
    zs = [z] + [lax.rem(z + i, 4) for i in (1, 2, 3)]
    ys = [y] + [lax.rem(y + i, 4) for i in (1, 2, 3)]
    ks = [k, lax.rem(k + 1, 2)]

    qcopy = pltpu.make_async_copy(q_ref, qv, qsem.at[0])
    qcopy.start()
    fcopies = {}
    for n, group in enumerate(GROUPS):
        for dk in (1, 0):
            for i, (dx, dz) in enumerate(group):
                a = ks[dk] * 16 + xs[dx] * 4 + zs[dz]
                rows = pl.ds(pl.multiple_of(a * 128, 128), 128)
                fcopies[n, dk, i] = pltpu.make_async_copy(
                    f_ref.at[rows], fv.at[n * 2 + dk, i], fsem.at[n * 2 + dk, i]
                )
    for dk in (1, 0):
        for i in range(4):
            fcopies[0, dk, i].start()

    grecv[...] = jnp.zeros_like(grecv)

    barrier = pltpu.get_barrier_semaphore()

    def greet(sem, dev):
        pl.semaphore_signal(sem, inc=1, device_id=dev, device_id_type=pl.DeviceIdType.MESH)

    greet(barrier, partner)
    for i in (1, 3, 2):
        greet(barrier, (y, z, xs[i], k))
        greet(barrier, (y, zs[i], x, k))
        greet(barrier, (ys[i], z, x, k))

    def hcopies(c):
        cols = pl.ds(pl.multiple_of(c * KCH, KCH), KCH)
        return (
            pltpu.make_async_copy(h_ref.at[:, cols], hv.at[c], hsem.at[0, c]),
            pltpu.make_async_copy(pi_ref.at[cols], piv.at[c], hsem.at[1, c]),
        )

    def gcopies(c):
        cols = pl.ds(pl.multiple_of(c * KCH, KCH), KCH)
        return (
            pltpu.make_async_copy(g_ref.at[:, cols], gv.at[c], gsem.at[0, c]),
            pltpu.make_async_copy(po_ref.at[cols], pov.at[c], gsem.at[1, c]),
        )

    qcopy.wait()
    for key, cp in fcopies.items():
        if key[0]:
            cp.start()
    for c in range(2):
        for cp in gcopies(c):
            cp.start()
    for c in range(7):
        for cp in hcopies(c):
            cp.start()
    qh, ql = split(qv[...])
    q3[0:512] = qh
    q3[512:1024] = ql
    q3[1024:1536] = qh

    def compute(n, dk):
        for i in range(4):
            fcopies[n, dk, i].wait()

        @pl.loop(0, 2)
        def _(i):
            pair = pl.ds(i * 2, 2)
            hi, lo = split(fv[n * 2 + dk, pair].reshape(256, 512))
            v = dot(jnp.concatenate([hi, hi, lo], axis=1), q3[...])
            uu[dk, n, pair] = v.reshape(2, 128, 256)

    done = []
    swaps = {}

    def swap(n):
        swaps[n] = remote(uu.at[1, n], cc.at[n], csend.at[n], crecv.at[n], partner)
        swaps[n].start()
        done.append(swaps[n])

    def merge(n):
        swaps[n].wait_recv()
        for i, (dx, dz) in enumerate(GROUPS[n]):
            v = uu[0, n, i] + cc[n, i]
            ua[dx, dz] = v[0:64]
            ub[dz, dx] = v[64:128]

    class Ring:
        def __init__(self, p, half, far, near, ids, plus, minus):
            self.p, self.half, self.far, self.near = p, half, far, near
            self.ids, self.plus, self.minus = ids, plus, minus
            self.recv = {}

        def piece(self, q, h):
            return self.p.at[q, pl.ds(h * self.half, self.half)]

        def go(self, name, n, src, dst, dev):
            cp = remote(src, dst, r_send.at[self.ids, n], r_recv.at[self.ids, n], dev)
            cp.start()
            self.recv[name] = cp
            done.append(cp)

        def send_far(self):
            self.go("f0", 0, self.piece(2, 0), self.far.at[0], self.plus)
            self.go("f1", 1, self.piece(2, 1), self.far.at[1], self.minus)

        def part(self, i, h):
            return self.near.at[i, pl.ds(h * self.half, self.half)]

        def send_plus_early(self):
            self.go("p1", 2, self.piece(1, 1), self.part(0, 1), self.plus)

        def send_minus_early(self):
            self.go("m0", 3, self.piece(3, 0), self.part(1, 0), self.minus)

        def relay(self):
            self.recv["f0"].wait_recv()
            s = self.piece(1, 0)
            s[...] = s[...] + self.far[0]
            self.go("p0", 4, s, self.part(0, 0), self.plus)
            self.recv["f1"].wait_recv()
            s = self.piece(3, 1)
            s[...] = s[...] + self.far[1]
            self.go("m1", 5, s, self.part(1, 1), self.minus)

        def finish(self):
            for name in ("p1", "m0", "p0", "m1"):
                self.recv[name].wait_recv()
            self.p[0] = self.p[0] + self.near[0] + self.near[1]

    ring_a = Ring(ua, 2, fa1, na1, 0, xp, xm)
    ring_b = Ring(ub, 2, fb1, nb1, 1, zp, zm)
    ring_a2 = Ring(ua.at[0], 32, fa2, na2, 2, zp, zm)
    ring_b2 = Ring(ub.at[0], 32, fb2, nb2, 3, xp, xm)

    compute(0, 1)
    pl.semaphore_wait(barrier, 10)
    for i in (1, 3, 2):
        greet(plane_sem, (y, zs[i], x, k))
    swap(0)
    compute(0, 0)
    compute(1, 1)
    swap(1)
    merge(0)
    ring_a.send_far()
    compute(1, 0)
    compute(2, 1)
    swap(2)
    merge(1)
    ring_b.send_far()
    compute(2, 0)
    compute(3, 1)
    swap(3)
    merge(2)
    ring_a.send_plus_early()
    ring_a.send_minus_early()
    ring_b.send_plus_early()
    ring_b.send_minus_early()
    compute(3, 0)
    pl.semaphore_wait(plane_sem, 3)
    for i in (1, 3, 2):
        greet(all_sem, (ys[i], z, x, k))

    mine = pl.ds(pl.multiple_of(k * 256, 256), 256)
    pg[mine] = jnp.zeros((256, 128), f32)
    pt[mine] = jnp.zeros((256, 128), f32)

    def proj(store, copies, a, b, first, end):
        @pl.loop(first, end)
        def _(c):
            for cp in copies(c):
                cp.wait()
            store[mine] = store[mine] + dot(a[c], b[c])

    proj(pg, gcopies, gv, pov, 0, 2)
    give_g = remote(pg.at[mine], pg.at[mine], psend.at[0], precv.at[0], partner)
    give_g.start()
    merge(3)
    proj(pt, hcopies, hv, piv, 0, 2)
    ring_a.relay()
    proj(pt, hcopies, hv, piv, 2, 4)
    ring_b.relay()
    proj(pt, hcopies, hv, piv, 4, 7)
    give_t = remote(pt.at[mine], pt.at[mine], psend.at[1], precv.at[1], partner)
    give_t.start()
    done.extend((give_g, give_t))

    off_row = off_ref[...].astype(f32)
    end_row = off_row + len_ref[...].astype(f32)
    off_col = jnp.transpose(jnp.broadcast_to(off_row, (8, 256)))[:, 0:1]
    end_col = jnp.transpose(jnp.broadcast_to(end_row, (8, 256)))[:, 0:1]
    slot0 = (chip * 512).astype(f32)
    slots = lax.broadcasted_iota(jnp.int32, (1, 512), 1).astype(f32) + slot0
    begun = jnp.sum((off_col <= slots).astype(f32), axis=0, keepdims=True)
    ended = jnp.sum((end_col <= slots).astype(f32), axis=0, keepdims=True)
    passed = jnp.sum((end_col <= slot0).astype(f32), axis=0, keepdims=True)
    window = jnp.where(begun == ended + 1.0, begun - 1.0 - passed, -1.0)
    member = (
        lax.broadcasted_iota(jnp.int32, (PITCH, 512), 0).astype(f32) == window
    ).astype(f32)

    give_g.wait_recv()
    give_t.wait_recv()
    pgt[...] = jnp.transpose(pg[...]).reshape(8, 16, 512)
    th, tl = split(pt[...])
    t2 = jnp.concatenate([th, tl], axis=1)

    def window_grads(half):
        lines = jnp.concatenate([pgt[half * 4 + k], pgt[half * 4 + 2 + k]], axis=0)
        spread = (lines[:, None, :] * member[None, :, :]).reshape(32 * PITCH, 512)
        hi, lo = split(spread)
        grads = []
        for i in (0, 256, 512):
            v = dot(hi[i : i + 256], t2)
            grads.append(v[:, 0:128] + v[:, 128:256] + dot(lo[i : i + 256], th))
        gsend[pl.ds(half * 32, 32)] = jnp.concatenate(grads, axis=0).reshape(32, PITCH, 128)

    window_grads(0)
    ring_a.finish()
    ring_a2.send_far()
    ring_a2.send_plus_early()
    ring_a2.send_minus_early()
    ring_b.finish()
    ring_b2.send_far()
    ring_b2.send_plus_early()
    ring_b2.send_minus_early()
    window_grads(1)
    pl.semaphore_wait(all_sem, 3)

    def spread_grads(p):
        oy = TURNS[p]
        for oz, ox in PLANE:
            if (oy, oz, ox) != (0, 0, 0):
                remote(
                    gsend.at[ys[oy] * 16 + xs[ox] * 4 + zs[oz], pl.ds(0, WIN)],
                    grecv.at[p * 16 + oz * 4 + ox, pl.ds(0, WIN)],
                    gssem.at[0], grsem.at[p], (ys[oy], zs[oz], xs[ox], k),
                ).start()

    for p in range(4):
        spread_grads(p)
    grecv[48] = gsend[y * 16 + x * 4 + z]
    ring_a2.relay()
    ring_b2.relay()

    cols = lax.broadcasted_iota(jnp.int32, (1, 64 * PITCH), 1)
    place = (cols * 2731) >> 16
    col_win = cols - place * PITCH
    turn = place >> 4
    from_y = y - jnp.where(turn == 0, 2, jnp.where(turn == 1, 1, jnp.where(turn == 2, 3, 0)))
    from_z = z - ((place >> 2) & 3)
    from_x = x - (place & 3)
    col_chip = (from_y & 3) * 16 + (from_z & 3) * 4 + (from_x & 3)
    col_slot = (col_chip * 512).astype(f32)
    before = jnp.sum((end_col <= col_slot).astype(f32), axis=0, keepdims=True)
    target = jnp.where(col_win < WIN, before + col_win.astype(f32), -1.0)
    line = lax.broadcasted_iota(jnp.int32, (512, 1), 0)
    sample = (line >> 3) * 4 + ((line >> 2) & 1) * 2 + (line & 1)
    oneh[...] = (sample.astype(f32) == target).astype(f32).astype(bf16)

    def gather_grads(first, count):
        for p in range(first // 16, (first + count) // 16):
            n = 15 if p == 3 else 16
            slots = grecv.at[pl.ds(p * 16, n), pl.ds(0, WIN)]
            pltpu.make_async_copy(slots, slots, grsem.at[p]).wait()
        part = pl.ds(first * PITCH, count * PITCH)
        gh, gl = split(grecv[first : first + count].reshape(count * PITCH, 128))
        gg = jnp.concatenate([gh, gl], axis=1)
        both = [dot(oneh[i : i + 256, part], gg) for i in (0, 256)]
        return [v[:, 0:128] + v[:, 128:256] for v in both]

    ring_a2.finish()
    ring_b2.finish()
    dense_a = gather_grads(0, 32)

    uh, ul = split(jnp.concatenate([ua[0, 0], ub[0, 0]], axis=0))
    u3 = jnp.concatenate([uh, ul, uh], axis=0)

    dense_b = gather_grads(32, 32)
    upper = ((line[0:256] >> 1) & 1) == 0
    for i in range(2):
        dh, dl = split(dense_a[i] + dense_b[i])
        both = dot(jnp.concatenate([dh, dh, dl], axis=1), u3)
        tiles = jnp.where(upper, both[:, 0:128], both[:, 128:256])
        sbuf[i * 32 : i * 32 + 32] = tiles.reshape(32, 8, 128)

    for oy, oz, ox in PEERS:
        for kk in range(2):
            remote(
                sbuf.at[ys[oy] * 16 + zs[oz] * 4 + xs[ox], pl.ds(kk * 4, 4)],
                srecv.at[k * 64 + chip, pl.ds(0, 4)],
                sssem.at[0], srsem.at[0], (ys[oy], zs[oz], xs[ox], kk),
            ).start()
    own = sbuf[chip]
    srecv[k * 64 + chip, 0:4] = jnp.where(k == 0, own[0:4], own[4:8])
    other[0:4] = jnp.where(k == 0, own[4:8], own[0:4])
    last = remote(
        other.at[pl.ds(0, 4)], srecv.at[k * 64 + chip, pl.ds(0, 4)],
        xsend.at[0], xsend.at[1], partner,
    )
    last.start()
    done.append(last)

    slots = srecv.at[pl.ds(0, 126), pl.ds(0, 4)]
    pltpu.make_async_copy(slots, slots, srsem.at[0]).wait()
    last.wait_recv()
    tile = jnp.sum(srecv[:, 0:4], axis=0)
    d = chip * 2 + k
    for s in range(2):
        n = lens_ref[2 * d + s].astype(f32)
        for j in range(2):
            line = tile[j * 2 + s : j * 2 + s + 1] * score_scale
            out_ref[s : s + 1, j * 128 : j * 128 + 128] = line / n

    for cp in done:
        cp.wait_send()
    sent = gsend.at[pl.ds(0, 63), pl.ds(0, WIN)]
    pltpu.make_async_copy(sent, sent, gssem.at[0]).wait()
    sent = sbuf.at[pl.ds(0, 63)]
    pltpu.make_async_copy(sent, sent, sssem.at[0]).wait()


def body(hidden_in, out_grad, proj_in, proj_out, inverse_fisher, queries, lengths, offsets):
    vmem = pltpu.VMEM
    dma = pltpu.SemaphoreType.DMA
    anys = pl.BlockSpec(memory_space=pl.ANY)
    invm = pl.BlockSpec(memory_space=pltpu.VMEM)
    return pl.pallas_call(
        kernel,
        out_shape=pltpu.VMEM((2, 256), f32),
        in_specs=[anys] * 6 + [invm] * 2 + [pl.BlockSpec(memory_space=pltpu.SMEM)],
        out_specs=invm,
        scratch_shapes=[
            vmem((8, 4, 128, 512), f32), vmem((512, 256), f32),
            vmem((7, 256, KCH), bf16), vmem((7, KCH, 128), bf16),
            vmem((2, 256, KCH), bf16), vmem((2, KCH, 128), bf16),
            vmem((1536, 256), bf16),
            vmem((2, 4, 4, 128, 256), f32), vmem((4, 4, 128, 256), f32),
            vmem((4, 4, 64, 256), f32), vmem((4, 4, 64, 256), f32),
            vmem((2, 2, 64, 256), f32), vmem((2, 2, 64, 256), f32),
            vmem((2, 4, 64, 256), f32), vmem((2, 4, 64, 256), f32),
            vmem((2, 32, 256), f32), vmem((2, 32, 256), f32),
            vmem((2, 64, 256), f32), vmem((2, 64, 256), f32),
            vmem((512, 128), f32), vmem((512, 128), f32), vmem((8, 16, 512), f32),
            vmem((64, PITCH, 128), f32), vmem((64, PITCH, 128), f32),
            vmem((512, 64 * PITCH), bf16),
            vmem((64, 8, 128), f32), vmem((128, 8, 128), f32), vmem((8, 128), f32),
            dma((8, 4)), dma((1,)), dma((2, 7)), dma((2, 2)),
            dma((4,)), dma((4,)), dma((4, 6)), dma((4, 6)),
            pltpu.SemaphoreType.REGULAR, pltpu.SemaphoreType.REGULAR,
            dma((2,)), dma((2,)), dma((1,)), dma((4,)), dma((1,)), dma((1,)),
            dma((2,)),
        ],
        compiler_params=pltpu.CompilerParams(
            collective_id=0, has_side_effects=True, vmem_limit_bytes=60 * 1024 * 1024
        ),
    )(
        inverse_fisher, queries, hidden_in, proj_in, out_grad, proj_out,
        offsets.reshape(1, 256), lengths.reshape(1, 256), lengths,
    )


def solution(mesh):
    whole = Mesh(mesh.devices.reshape(4, 4, 4, 2), AXES)
    col = AXES[1:]
    return jax.shard_map(
        body,
        mesh=whole,
        in_specs=(
            P(AXES, None), P(AXES, None), P(), P(), P("row", col), P(col, None), P(), P(),
        ),
        out_specs=P(AXES, None),
        check_vma=False,
    )
```

```python
import jax
import jax.numpy as jnp
from jax import lax
from jax.experimental import pallas as pl
from jax.experimental.pallas import tpu as pltpu
from jax.sharding import Mesh
from jax.sharding import PartitionSpec as P

AXES = ("row", "col_0", "col_1", "col_2")
WIN = 17
PITCH = 24
KCH = 2048
GROUPS = (
    ((2, 2), (2, 0)), ((0, 2), (2, 1)), ((2, 3), (3, 2)), ((1, 2), (1, 3)),
    ((3, 0), (3, 1)), ((0, 3), (1, 1)), ((1, 0), (3, 3)), ((0, 1), (0, 0)),
)
PEERS = sorted(
    ((i // 16, i // 4 % 4, i % 4) for i in range(1, 64)),
    key=lambda o: -sum(min(v, 4 - v) for v in o),
)
PLANE = ((2, 2), (2, 1), (1, 2), (2, 3), (3, 2), (1, 1), (1, 3), (3, 1), (3, 3),
         (0, 2), (2, 0), (0, 1), (1, 0), (0, 3), (3, 0), (0, 0))
TURNS = (2, 1, 3, 0)
score_scale = 0.0625
f32 = jnp.float32
bf16 = jnp.bfloat16


def split(v):
    hi = v.astype(bf16)
    lo = (v - hi.astype(f32)).astype(bf16)
    return hi, lo


def dot(a, b):
    return jnp.dot(a, b, preferred_element_type=f32)


def kernel(
    f_ref, q_ref, h_ref, pi_ref, g_ref, po_ref, off_hbm, len_hbm,
    out_ref,
    fv, qv, hv, piv, gv, pov, q3,
    uu, cc, ua, ub,
    fa1, fb1, na1, nb1, fa2, fb2, na2, nb2,
    pt, pg, pgt, gsend, grecv, oneh, sbuf, srecv, other,
    off_ref, len_ref, fsem, qsem, lsem, hsem, gsem,
    csend, crecv, r_send, r_recv,
    plane_sem, all_sem, psend, precv, gssem, grsem, sssem, srsem, xsend,
):
    y = lax.axis_index("row")
    z = lax.axis_index("col_0")
    x = lax.axis_index("col_1")
    k = lax.axis_index("col_2")
    chip = y * 16 + z * 4 + x

    def remote(src, dst, ss, rs, dev):
        return pltpu.make_async_remote_copy(
            src_ref=src, dst_ref=dst, send_sem=ss, recv_sem=rs,
            device_id=dev, device_id_type=pl.DeviceIdType.MESH,
        )

    partner = (y, z, x, lax.rem(k + 1, 2))
    xp = (y, z, lax.rem(x + 1, 4), k)
    xm = (y, z, lax.rem(x + 3, 4), k)
    zp = (y, lax.rem(z + 1, 4), x, k)
    zm = (y, lax.rem(z + 3, 4), x, k)

    xs = [x] + [lax.rem(x + i, 4) for i in (1, 2, 3)]
    zs = [z] + [lax.rem(z + i, 4) for i in (1, 2, 3)]
    ys = [y] + [lax.rem(y + i, 4) for i in (1, 2, 3)]
    ks = [k, lax.rem(k + 1, 2)]

    qcopy = pltpu.make_async_copy(q_ref, qv, qsem.at[0])
    qcopy.start()
    fcopies = {}
    for n, group in enumerate(GROUPS):
        for dk in (1, 0):
            for i, (dx, dz) in enumerate(group):
                a = ks[dk] * 16 + xs[dx] * 4 + zs[dz]
                rows = pl.ds(pl.multiple_of(a * 128, 128), 128)
                fcopies[n, dk, i] = pltpu.make_async_copy(
                    f_ref.at[rows], fv.at[n * 2 + dk, i], fsem.at[n * 2 + dk, i]
                )
    for dk in (1, 0):
        for i in range(2):
            fcopies[0, dk, i].start()

    lcopies = (
        pltpu.make_async_copy(off_hbm, off_ref, lsem.at[0]),
        pltpu.make_async_copy(len_hbm, len_ref, lsem.at[1]),
    )
    for cp in lcopies:
        cp.start()

    grecv[...] = jnp.zeros_like(grecv)

    barrier = pltpu.get_barrier_semaphore()

    def greet(sem, dev):
        pl.semaphore_signal(sem, inc=1, device_id=dev, device_id_type=pl.DeviceIdType.MESH)

    greet(barrier, partner)
    for i in (1, 3, 2):
        greet(barrier, (y, z, xs[i], k))
        greet(barrier, (y, zs[i], x, k))
        greet(barrier, (ys[i], z, x, k))

    def hcopies(c):
        cols = pl.ds(pl.multiple_of(c * KCH, KCH), KCH)
        return (
            pltpu.make_async_copy(h_ref.at[:, cols], hv.at[c], hsem.at[0, c]),
            pltpu.make_async_copy(pi_ref.at[cols], piv.at[c], hsem.at[1, c]),
        )

    def gcopies(c):
        cols = pl.ds(pl.multiple_of(c * KCH, KCH), KCH)
        return (
            pltpu.make_async_copy(g_ref.at[:, cols], gv.at[c], gsem.at[0, c]),
            pltpu.make_async_copy(po_ref.at[cols], pov.at[c], gsem.at[1, c]),
        )

    qcopy.wait()
    for key, cp in fcopies.items():
        if key[0]:
            cp.start()
    for c in range(2):
        for cp in gcopies(c):
            cp.start()
    for c in range(7):
        for cp in hcopies(c):
            cp.start()
    qh, ql = split(qv[...])
    q3[0:512] = qh
    q3[512:1024] = ql
    q3[1024:1536] = qh

    def compute(n, dk):
        for i in range(2):
            fcopies[n, dk, i].wait()

        @pl.when(y >= 0)
        def _():
            hi, lo = split(fv[n * 2 + dk].reshape(256, 512))
            v = dot(jnp.concatenate([hi, hi, lo], axis=1), q3[...])
            uu[dk, n] = v.reshape(2, 128, 256)

    done = []
    swaps = {}

    def swap(n):
        swaps[n] = remote(uu.at[1, n], cc.at[n], csend.at[n], crecv.at[n], partner)
        swaps[n].start()
        done.append(swaps[n])

    def merge(n):
        swaps[n].wait_recv()
        for i, (dx, dz) in enumerate(GROUPS[n]):
            v = uu[0, n, i] + cc[n, i]
            ua[dx, dz] = v[0:64]
            ub[dz, dx] = v[64:128]

    class Ring:
        def __init__(self, p, half, far, near, ids, plus, minus):
            self.p, self.half, self.far, self.near = p, half, far, near
            self.ids, self.plus, self.minus = ids, plus, minus
            self.copies = {"far0": [], "far1": [], "near": []}
            self.count = 0

        def go(self, group, q, first, size, dst, dev):
            n = self.count
            self.count += 1
            cp = remote(
                self.p.at[q, pl.ds(first, size)], dst.at[pl.ds(first, size)],
                r_send.at[self.ids, n], r_recv.at[self.ids, n], dev,
            )
            cp.start()
            self.copies[group].append(cp)
            done.append(cp)

        def send_far(self, first, size):
            h = first // self.half
            self.go(f"far{h}", 2, first, size, self.far, self.minus if h else self.plus)

        def send_plus(self, first, size):
            self.go("near", 1, first, size, self.near.at[0], self.plus)

        def send_minus(self, first, size):
            self.go("near", 3, first, size, self.near.at[1], self.minus)

        def send_own(self):
            for h in range(2):
                self.send_far(h * self.half, self.half)
            self.send_plus(self.half, self.half)
            self.send_minus(0, self.half)

        def relay(self):
            for h, q in ((0, 1), (1, 3)):
                for cp in self.copies[f"far{h}"]:
                    cp.wait_recv()
                part = pl.ds(h * self.half, self.half)
                self.p[q, part] = self.p[q, part] + self.far[part]
                (self.send_minus if h else self.send_plus)(h * self.half, self.half)

        def finish(self):
            for cp in self.copies["near"]:
                cp.wait_recv()
            self.p[0] = self.p[0] + self.near[0] + self.near[1]

    ring_a = Ring(ua, 2, fa1, na1, 0, xp, xm)
    ring_b = Ring(ub, 2, fb1, nb1, 1, zp, zm)
    ring_a2 = Ring(ua.at[0], 32, fa2, na2, 2, zp, zm)
    ring_b2 = Ring(ub.at[0], 32, fb2, nb2, 3, xp, xm)

    compute(0, 1)
    pl.semaphore_wait(barrier, 10)
    for i in (1, 3, 2):
        greet(plane_sem, (y, zs[i], x, k))
    swap(0)
    compute(0, 0)
    compute(1, 1)
    swap(1)
    compute(1, 0)
    merge(0)
    ring_a.send_far(2, 1)
    ring_b.send_far(2, 1)
    ring_a.send_far(0, 1)
    compute(2, 1)
    swap(2)
    compute(2, 0)
    merge(1)
    ring_b.send_far(0, 1)
    ring_a.send_far(1, 1)
    compute(3, 1)
    swap(3)
    compute(3, 0)
    merge(2)
    ring_a.send_far(3, 1)
    ring_b.send_far(3, 1)
    compute(4, 1)
    swap(4)
    compute(4, 0)
    merge(3)
    ring_b.send_far(1, 1)
    ring_a.send_plus(2, 2)
    ring_b.send_minus(1, 1)
    compute(5, 1)
    swap(5)
    compute(5, 0)
    merge(4)
    ring_a.send_minus(0, 2)
    ring_b.send_plus(2, 2)
    compute(6, 1)
    swap(6)
    compute(6, 0)
    merge(5)
    ring_b.send_minus(0, 1)
    compute(7, 1)
    swap(7)
    compute(7, 0)
    merge(6)
    pl.semaphore_wait(plane_sem, 3)
    for i in (1, 3, 2):
        greet(all_sem, (ys[i], z, x, k))

    mine = pl.ds(pl.multiple_of(k * 256, 256), 256)
    pg[mine] = jnp.zeros((256, 128), f32)
    pt[mine] = jnp.zeros((256, 128), f32)

    def proj(store, copies, a, b, first, end):
        @pl.loop(first, end)
        def _(c):
            for cp in copies(c):
                cp.wait()
            store[mine] = store[mine] + dot(a[c], b[c])

    ring_a.relay()
    proj(pg, gcopies, gv, pov, 0, 2)
    merge(7)
    give_g = remote(pg.at[mine], pg.at[mine], psend.at[0], precv.at[0], partner)
    give_g.start()
    ring_b.relay()
    proj(pt, hcopies, hv, piv, 0, 7)
    give_t = remote(pt.at[mine], pt.at[mine], psend.at[1], precv.at[1], partner)
    give_t.start()
    done.extend((give_g, give_t))

    for cp in lcopies:
        cp.wait()
    off_row = off_ref[...].astype(f32)
    end_row = off_row + len_ref[...].astype(f32)
    off_col = jnp.transpose(jnp.broadcast_to(off_row, (8, 256)))[:, 0:1]
    end_col = jnp.transpose(jnp.broadcast_to(end_row, (8, 256)))[:, 0:1]
    slot0 = (chip * 512).astype(f32)
    slots = lax.broadcasted_iota(jnp.int32, (1, 512), 1).astype(f32) + slot0
    begun = jnp.sum((off_col <= slots).astype(f32), axis=0, keepdims=True)
    ended = jnp.sum((end_col <= slots).astype(f32), axis=0, keepdims=True)
    passed = jnp.sum((end_col <= slot0).astype(f32), axis=0, keepdims=True)
    window = jnp.where(begun == ended + 1.0, begun - 1.0 - passed, -1.0)
    member = (
        lax.broadcasted_iota(jnp.int32, (PITCH, 512), 0).astype(f32) == window
    ).astype(f32)

    def window_grads(first, member_here, add):
        here = pl.ds(pl.multiple_of(first, 256), 256)
        turned = jnp.transpose(pg[here])
        pgt[...] = turned.reshape(8, 16, 256)
        th, tl = split(pt[here])
        t2 = jnp.concatenate([th, tl], axis=1)
        for half in range(2):
            lines = jnp.concatenate([pgt[half * 4 + k], pgt[half * 4 + 2 + k]], axis=0)
            spread = (lines[:, None, :] * member_here[None, :, :]).reshape(32 * PITCH, 256)
            hi, lo = split(spread)
            grads = []
            for i in (0, 256, 512):
                v = dot(hi[i : i + 256], t2)
                grads.append(v[:, 0:128] + v[:, 128:256] + dot(lo[i : i + 256], th))
            total = jnp.concatenate(grads, axis=0).reshape(32, PITCH, 128)
            part = pl.ds(half * 32, 32)
            gsend[part] = gsend[part] + total if add else total

    window_grads(k * 256, jnp.where(k == 0, member[:, 0:256], member[:, 256:512]), False)
    give_g.wait_recv()
    give_t.wait_recv()
    away = ks[1]
    window_grads(away * 256, jnp.where(k == 0, member[:, 256:512], member[:, 0:256]), True)
    pl.semaphore_wait(all_sem, 3)

    def spread_grads(p):
        oy = TURNS[p]
        for oz, ox in PLANE:
            if (oy, oz, ox) != (0, 0, 0):
                remote(
                    gsend.at[ys[oy] * 16 + xs[ox] * 4 + zs[oz], pl.ds(0, WIN)],
                    grecv.at[p * 16 + oz * 4 + ox, pl.ds(0, WIN)],
                    gssem.at[0], grsem.at[p], (ys[oy], zs[oz], xs[ox], k),
                ).start()

    ring_a.finish()
    ring_a2.send_own()
    ring_b.finish()
    ring_b2.send_own()
    spread_grads(0)
    spread_grads(1)
    spread_grads(2)
    spread_grads(3)
    grecv[48] = gsend[y * 16 + x * 4 + z]
    ring_a2.relay()
    ring_b2.relay()

    cols = lax.broadcasted_iota(jnp.int32, (1, 64 * PITCH), 1)
    place = (cols * 2731) >> 16
    col_win = cols - place * PITCH
    turn = place >> 4
    from_y = y - jnp.where(turn == 0, 2, jnp.where(turn == 1, 1, jnp.where(turn == 2, 3, 0)))
    from_z = z - ((place >> 2) & 3)
    from_x = x - (place & 3)
    col_chip = (from_y & 3) * 16 + (from_z & 3) * 4 + (from_x & 3)
    col_slot = (col_chip * 512).astype(f32)
    before = jnp.sum((end_col <= col_slot).astype(f32), axis=0, keepdims=True)
    target = jnp.where(col_win < WIN, before + col_win.astype(f32), -1.0)
    line = lax.broadcasted_iota(jnp.int32, (512, 1), 0)
    sample = (line >> 3) * 4 + ((line >> 2) & 1) * 2 + (line & 1)
    oneh[...] = (sample.astype(f32) == target).astype(f32).astype(bf16)

    def gather_grads(first, count):
        for p in range(first // 16, (first + count) // 16):
            n = 15 if p == 3 else 16
            slots = grecv.at[pl.ds(p * 16, n), pl.ds(0, WIN)]
            pltpu.make_async_copy(slots, slots, grsem.at[p]).wait()
        part = pl.ds(first * PITCH, count * PITCH)
        gh, gl = split(grecv[first : first + count].reshape(count * PITCH, 128))
        gg = jnp.concatenate([gh, gl], axis=1)
        both = [dot(oneh[i : i + 256, part], gg) for i in (0, 256)]
        return [v[:, 0:128] + v[:, 128:256] for v in both]

    ring_a2.finish()
    ring_b2.finish()
    dense_a = gather_grads(0, 32)

    uh, ul = split(jnp.concatenate([ua[0, 0], ub[0, 0]], axis=0))
    u3 = jnp.concatenate([uh, ul, uh], axis=0)

    dense_b = gather_grads(32, 32)
    upper = ((line[0:256] >> 1) & 1) == 0
    for i in range(2):
        dh, dl = split(dense_a[i] + dense_b[i])
        both = dot(jnp.concatenate([dh, dh, dl], axis=1), u3)
        tiles = jnp.where(upper, both[:, 0:128], both[:, 128:256])
        sbuf[i * 32 : i * 32 + 32] = tiles.reshape(32, 8, 128)

    for oy, oz, ox in PEERS:
        for kk in range(2):
            remote(
                sbuf.at[ys[oy] * 16 + zs[oz] * 4 + xs[ox], pl.ds(kk * 4, 4)],
                srecv.at[k * 64 + chip, pl.ds(0, 4)],
                sssem.at[0], srsem.at[0], (ys[oy], zs[oz], xs[ox], kk),
            ).start()
    own = sbuf[chip]
    srecv[k * 64 + chip, 0:4] = jnp.where(k == 0, own[0:4], own[4:8])
    other[0:4] = jnp.where(k == 0, own[4:8], own[0:4])
    last = remote(
        other.at[pl.ds(0, 4)], srecv.at[k * 64 + chip, pl.ds(0, 4)],
        xsend.at[0], xsend.at[1], partner,
    )
    last.start()
    done.append(last)

    slots = srecv.at[pl.ds(0, 126), pl.ds(0, 4)]
    pltpu.make_async_copy(slots, slots, srsem.at[0]).wait()
    last.wait_recv()
    tile = jnp.sum(srecv[:, 0:4], axis=0)
    d = chip * 2 + k
    for s in range(2):
        here = lax.broadcasted_iota(jnp.int32, (1, 256), 1) == 2 * d + s
        n = jnp.sum(jnp.where(here, len_ref[...], 0).astype(f32), axis=1, keepdims=True)
        for j in range(2):
            line = tile[j * 2 + s : j * 2 + s + 1] * score_scale
            out_ref[s : s + 1, j * 128 : j * 128 + 128] = line / n

    for cp in done:
        cp.wait_send()
    sent = gsend.at[pl.ds(0, 63), pl.ds(0, WIN)]
    pltpu.make_async_copy(sent, sent, gssem.at[0]).wait()
    sent = sbuf.at[pl.ds(0, 63)]
    pltpu.make_async_copy(sent, sent, sssem.at[0]).wait()


def body(hidden_in, out_grad, proj_in, proj_out, inverse_fisher, queries, lengths, offsets):
    vmem = pltpu.VMEM
    dma = pltpu.SemaphoreType.DMA
    anys = pl.BlockSpec(memory_space=pl.ANY)
    invm = pl.BlockSpec(memory_space=pltpu.VMEM)
    return pl.pallas_call(
        kernel,
        out_shape=pltpu.VMEM((2, 256), f32),
        in_specs=[anys] * 8,
        out_specs=invm,
        scratch_shapes=[
            vmem((16, 2, 128, 512), f32), vmem((512, 256), f32),
            vmem((7, 256, KCH), bf16), vmem((7, KCH, 128), bf16),
            vmem((2, 256, KCH), bf16), vmem((2, KCH, 128), bf16),
            vmem((1536, 256), bf16),
            vmem((2, 8, 2, 128, 256), f32), vmem((8, 2, 128, 256), f32),
            vmem((4, 4, 64, 256), f32), vmem((4, 4, 64, 256), f32),
            vmem((4, 64, 256), f32), vmem((4, 64, 256), f32),
            vmem((2, 4, 64, 256), f32), vmem((2, 4, 64, 256), f32),
            vmem((64, 256), f32), vmem((64, 256), f32),
            vmem((2, 64, 256), f32), vmem((2, 64, 256), f32),
            vmem((512, 128), f32), vmem((512, 128), f32), vmem((8, 16, 256), f32),
            vmem((64, PITCH, 128), f32), vmem((64, PITCH, 128), f32),
            vmem((512, 64 * PITCH), bf16),
            vmem((64, 8, 128), f32), vmem((128, 8, 128), f32), vmem((8, 128), f32),
            vmem((1, 256), jnp.int32), vmem((1, 256), jnp.int32),
            dma((16, 2)), dma((1,)), dma((2,)), dma((2, 7)), dma((2, 2)),
            dma((8,)), dma((8,)), dma((4, 10)), dma((4, 10)),
            pltpu.SemaphoreType.REGULAR, pltpu.SemaphoreType.REGULAR,
            dma((2,)), dma((2,)), dma((1,)), dma((4,)), dma((1,)), dma((1,)),
            dma((2,)),
        ],
        compiler_params=pltpu.CompilerParams(
            collective_id=0, has_side_effects=True, vmem_limit_bytes=60 * 1024 * 1024
        ),
    )(
        inverse_fisher, queries, hidden_in, proj_in, out_grad, proj_out,
        offsets.reshape(1, 256), lengths.reshape(1, 256),
    )


def solution(mesh):
    whole = Mesh(mesh.devices.reshape(4, 4, 4, 2), AXES)
    col = AXES[1:]
    return jax.shard_map(
        body,
        mesh=whole,
        in_specs=(
            P(AXES, None), P(AXES, None), P(), P(), P("row", col), P(col, None), P(), P(),
        ),
        out_specs=P(AXES, None),
        check_vma=False,
    )
```

```python
import jax
import jax.numpy as jnp
from jax import lax
from jax.experimental import pallas as pl
from jax.experimental.pallas import tpu as pltpu
from jax.sharding import Mesh
from jax.sharding import PartitionSpec as P

AXES = ("row", "col_0", "col_1", "col_2")
WIN = 17
PITCH = 24
KCH = 2048
GROUPS = (
    ((2, 2), (2, 0)), ((0, 2), (2, 1)), ((2, 3), (3, 2)), ((1, 2), (1, 3)),
    ((3, 0), (3, 1)), ((0, 3), (1, 1)), ((1, 0), (3, 3)), ((0, 1), (0, 0)),
)
PLANE = ((2, 2), (2, 1), (1, 2), (2, 3), (3, 2), (1, 1), (1, 3), (3, 1), (3, 3),
         (0, 2), (2, 0), (0, 1), (1, 0), (0, 3), (3, 0), (0, 0))
TURNS = (2, 1, 3, 0)
score_scale = 0.0625
f32 = jnp.float32
bf16 = jnp.bfloat16


def split(v):
    hi = v.astype(bf16)
    lo = (v - hi.astype(f32)).astype(bf16)
    return hi, lo


def dot(a, b):
    return jnp.dot(a, b, preferred_element_type=f32)


def kernel(
    f_ref, q_ref, h_ref, pi_ref, g_ref, po_ref, off_hbm, len_hbm,
    out_ref,
    fv, qv, hv, piv, gv, pov, q3,
    uu, cc, ua, ub,
    fa1, fb1, na1, nb1, fa2, fb2, na2, nb2,
    pt, pg, pgt, gsend, grecv, oneh, sbuf, srecv, other,
    off_ref, len_ref, fsem, qsem, lsem, hsem, gsem,
    csend, crecv, r_send, r_recv,
    plane_sem, all_sem, psend, precv, gssem, grsem, sssem, srsem, xsend,
):
    y = lax.axis_index("row")
    z = lax.axis_index("col_0")
    x = lax.axis_index("col_1")
    k = lax.axis_index("col_2")
    chip = y * 16 + z * 4 + x

    def remote(src, dst, ss, rs, dev):
        return pltpu.make_async_remote_copy(
            src_ref=src, dst_ref=dst, send_sem=ss, recv_sem=rs,
            device_id=dev, device_id_type=pl.DeviceIdType.MESH,
        )

    partner = (y, z, x, lax.rem(k + 1, 2))
    xp = (y, z, lax.rem(x + 1, 4), k)
    xm = (y, z, lax.rem(x + 3, 4), k)
    zp = (y, lax.rem(z + 1, 4), x, k)
    zm = (y, lax.rem(z + 3, 4), x, k)

    xs = [x] + [lax.rem(x + i, 4) for i in (1, 2, 3)]
    zs = [z] + [lax.rem(z + i, 4) for i in (1, 2, 3)]
    ys = [y] + [lax.rem(y + i, 4) for i in (1, 2, 3)]
    ks = [k, lax.rem(k + 1, 2)]

    qcopy = pltpu.make_async_copy(q_ref, qv, qsem.at[0])
    qcopy.start()
    fcopies = {}
    for n, group in enumerate(GROUPS):
        for dk in (1, 0):
            for i, (dx, dz) in enumerate(group):
                a = ks[dk] * 16 + xs[dx] * 4 + zs[dz]
                rows = pl.ds(pl.multiple_of(a * 128, 128), 128)
                fcopies[n, dk, i] = pltpu.make_async_copy(
                    f_ref.at[rows], fv.at[n * 2 + dk, i], fsem.at[n * 2 + dk, i]
                )
    for dk in (1, 0):
        for i in range(2):
            fcopies[0, dk, i].start()

    lcopies = (
        pltpu.make_async_copy(off_hbm, off_ref, lsem.at[0]),
        pltpu.make_async_copy(len_hbm, len_ref, lsem.at[1]),
    )
    for cp in lcopies:
        cp.start()

    grecv[...] = jnp.zeros_like(grecv)

    barrier = pltpu.get_barrier_semaphore()

    def greet(sem, dev):
        pl.semaphore_signal(sem, inc=1, device_id=dev, device_id_type=pl.DeviceIdType.MESH)

    greet(barrier, partner)
    for i in (1, 3, 2):
        greet(barrier, (y, z, xs[i], k))
        greet(barrier, (y, zs[i], x, k))
        greet(barrier, (ys[i], z, x, k))

    def hcopies(c):
        cols = pl.ds(pl.multiple_of(c * KCH, KCH), KCH)
        return (
            pltpu.make_async_copy(h_ref.at[:, cols], hv.at[c], hsem.at[0, c]),
            pltpu.make_async_copy(pi_ref.at[cols], piv.at[c], hsem.at[1, c]),
        )

    def gcopies(c):
        cols = pl.ds(pl.multiple_of(c * KCH, KCH), KCH)
        return (
            pltpu.make_async_copy(g_ref.at[:, cols], gv.at[c], gsem.at[0, c]),
            pltpu.make_async_copy(po_ref.at[cols], pov.at[c], gsem.at[1, c]),
        )

    qcopy.wait()
    for key, cp in fcopies.items():
        if key[0]:
            cp.start()
    for c in range(2):
        for cp in gcopies(c):
            cp.start()
    for c in range(7):
        for cp in hcopies(c):
            cp.start()
    qh, ql = split(qv[...])
    q3[0:512] = qh
    q3[512:1024] = ql
    q3[1024:1536] = qh

    def compute(n, dk):
        for i in range(2):
            fcopies[n, dk, i].wait()

        @pl.when(y >= 0)
        def _():
            hi, lo = split(fv[n * 2 + dk].reshape(256, 512))
            v = dot(jnp.concatenate([hi, hi, lo], axis=1), q3[...])
            uu[dk, n] = v.reshape(2, 128, 256)

    done = []
    swaps = {}

    def swap(n):
        swaps[n] = remote(uu.at[1, n], cc.at[n], csend.at[n], crecv.at[n], partner)
        swaps[n].start()
        done.append(swaps[n])

    def merge(n):
        swaps[n].wait_recv()
        for i, (dx, dz) in enumerate(GROUPS[n]):
            v = uu[0, n, i] + cc[n, i]
            ua[dx, dz] = v[0:64]
            ub[dz, dx] = v[64:128]

    class Ring:
        def __init__(self, p, half, far, near, ids, plus, minus):
            self.p, self.half, self.far, self.near = p, half, far, near
            self.ids, self.plus, self.minus = ids, plus, minus
            self.copies = {"far0": [], "far1": [], "near": []}
            self.count = 0

        def go(self, group, q, first, size, dst, dev):
            n = self.count
            self.count += 1
            cp = remote(
                self.p.at[q, pl.ds(first, size)], dst.at[pl.ds(first, size)],
                r_send.at[self.ids, n], r_recv.at[self.ids, n], dev,
            )
            cp.start()
            self.copies[group].append(cp)
            done.append(cp)

        def send_far(self, first, size):
            h = first // self.half
            self.go(f"far{h}", 2, first, size, self.far, self.minus if h else self.plus)

        def send_plus(self, first, size):
            self.go("near", 1, first, size, self.near.at[0], self.plus)

        def send_minus(self, first, size):
            self.go("near", 3, first, size, self.near.at[1], self.minus)

        def send_own(self):
            for h in range(2):
                self.send_far(h * self.half, self.half)
            self.send_plus(self.half, self.half)
            self.send_minus(0, self.half)

        def relay(self):
            for h, q in ((0, 1), (1, 3)):
                for cp in self.copies[f"far{h}"]:
                    cp.wait_recv()
                part = pl.ds(h * self.half, self.half)
                self.p[q, part] = self.p[q, part] + self.far[part]
                (self.send_minus if h else self.send_plus)(h * self.half, self.half)

        def finish(self):
            for cp in self.copies["near"]:
                cp.wait_recv()
            self.p[0] = self.p[0] + self.near[0] + self.near[1]

    ring_a = Ring(ua, 2, fa1, na1, 0, xp, xm)
    ring_b = Ring(ub, 2, fb1, nb1, 1, zp, zm)
    ring_a2 = Ring(ua.at[0], 32, fa2, na2, 2, zp, zm)
    ring_b2 = Ring(ub.at[0], 32, fb2, nb2, 3, xp, xm)

    compute(0, 1)
    pl.semaphore_wait(barrier, 10)
    for i in (1, 3, 2):
        greet(plane_sem, (y, zs[i], x, k))
    swap(0)
    compute(0, 0)
    compute(1, 1)
    swap(1)
    compute(1, 0)
    merge(0)
    ring_a.send_far(2, 1)
    ring_b.send_far(2, 1)
    ring_a.send_far(0, 1)
    compute(2, 1)
    swap(2)
    compute(2, 0)
    merge(1)
    ring_b.send_far(0, 1)
    ring_a.send_far(1, 1)
    compute(3, 1)
    swap(3)
    compute(3, 0)
    merge(2)
    ring_a.send_far(3, 1)
    ring_b.send_far(3, 1)
    compute(4, 1)
    swap(4)
    compute(4, 0)
    merge(3)
    ring_b.send_far(1, 1)
    ring_a.send_plus(2, 2)
    ring_b.send_minus(1, 1)
    compute(5, 1)
    swap(5)
    compute(5, 0)
    merge(4)
    ring_a.send_minus(0, 2)
    ring_b.send_plus(2, 2)
    compute(6, 1)
    swap(6)
    compute(6, 0)
    merge(5)
    ring_b.send_minus(0, 1)
    compute(7, 1)
    swap(7)
    compute(7, 0)
    merge(6)
    pl.semaphore_wait(plane_sem, 3)
    for i in (1, 3, 2):
        greet(all_sem, (ys[i], z, x, k))

    mine = pl.ds(pl.multiple_of(k * 256, 256), 256)
    pg[mine] = jnp.zeros((256, 128), f32)
    pt[mine] = jnp.zeros((256, 128), f32)

    def proj(store, copies, a, b, first, end):
        @pl.loop(first, end)
        def _(c):
            for cp in copies(c):
                cp.wait()
            store[mine] = store[mine] + dot(a[c], b[c])

    ring_a.relay()
    proj(pg, gcopies, gv, pov, 0, 2)
    merge(7)
    give_g = remote(pg.at[mine], pg.at[mine], psend.at[0], precv.at[0], partner)
    give_g.start()
    ring_b.relay()
    proj(pt, hcopies, hv, piv, 0, 7)
    give_t = remote(pt.at[mine], pt.at[mine], psend.at[1], precv.at[1], partner)
    give_t.start()
    done.extend((give_g, give_t))

    for cp in lcopies:
        cp.wait()
    off_row = off_ref[...].astype(f32)
    end_row = off_row + len_ref[...].astype(f32)
    off_col = jnp.transpose(jnp.broadcast_to(off_row, (8, 256)))[:, 0:1]
    end_col = jnp.transpose(jnp.broadcast_to(end_row, (8, 256)))[:, 0:1]
    slot0 = (chip * 512).astype(f32)
    slots = lax.broadcasted_iota(jnp.int32, (1, 512), 1).astype(f32) + slot0
    begun = jnp.sum((off_col <= slots).astype(f32), axis=0, keepdims=True)
    ended = jnp.sum((end_col <= slots).astype(f32), axis=0, keepdims=True)
    passed = jnp.sum((end_col <= slot0).astype(f32), axis=0, keepdims=True)
    window = jnp.where(begun == ended + 1.0, begun - 1.0 - passed, -1.0)
    member = (
        lax.broadcasted_iota(jnp.int32, (PITCH, 512), 0).astype(f32) == window
    ).astype(f32)

    def window_grads(first, member_here, add):
        here = pl.ds(pl.multiple_of(first, 256), 256)
        turned = jnp.transpose(pg[here])
        pgt[...] = turned.reshape(8, 16, 256)
        th, tl = split(pt[here])
        t2 = jnp.concatenate([th, tl], axis=1)
        for half in range(2):
            lines = jnp.concatenate([pgt[half * 4 + k], pgt[half * 4 + 2 + k]], axis=0)
            spread = (lines[:, None, :] * member_here[None, :, :]).reshape(32 * PITCH, 256)
            hi, lo = split(spread)
            grads = []
            for i in (0, 256, 512):
                v = dot(hi[i : i + 256], t2)
                grads.append(v[:, 0:128] + v[:, 128:256] + dot(lo[i : i + 256], th))
            total = jnp.concatenate(grads, axis=0).reshape(32, PITCH, 128)
            part = pl.ds(half * 32, 32)
            gsend[part] = gsend[part] + total if add else total

    window_grads(k * 256, jnp.where(k == 0, member[:, 0:256], member[:, 256:512]), False)
    give_g.wait_recv()
    give_t.wait_recv()
    away = ks[1]
    window_grads(away * 256, jnp.where(k == 0, member[:, 256:512], member[:, 0:256]), True)
    pl.semaphore_wait(all_sem, 3)

    def spread_grads(p):
        oy = TURNS[p]
        for oz, ox in PLANE:
            if (oy, oz, ox) != (0, 0, 0):
                remote(
                    gsend.at[ys[oy] * 16 + xs[ox] * 4 + zs[oz], pl.ds(0, WIN)],
                    grecv.at[p * 16 + oz * 4 + ox, pl.ds(0, WIN)],
                    gssem.at[0], grsem.at[p], (ys[oy], zs[oz], xs[ox], k),
                ).start()

    ring_a.finish()
    ring_a2.send_own()
    ring_b.finish()
    ring_b2.send_own()
    spread_grads(0)
    spread_grads(1)
    spread_grads(2)
    spread_grads(3)
    grecv[48] = gsend[y * 16 + x * 4 + z]
    ring_a2.relay()
    ring_b2.relay()

    cols = lax.broadcasted_iota(jnp.int32, (1, 64 * PITCH), 1)
    place = (cols * 2731) >> 16
    col_win = cols - place * PITCH
    turn = place >> 4
    from_y = y - jnp.where(turn == 0, 2, jnp.where(turn == 1, 1, jnp.where(turn == 2, 3, 0)))
    from_z = z - ((place >> 2) & 3)
    from_x = x - (place & 3)
    col_chip = (from_y & 3) * 16 + (from_z & 3) * 4 + (from_x & 3)
    col_slot = (col_chip * 512).astype(f32)
    before = jnp.sum((end_col <= col_slot).astype(f32), axis=0, keepdims=True)
    target = jnp.where(col_win < WIN, before + col_win.astype(f32), -1.0)
    line = lax.broadcasted_iota(jnp.int32, (512, 1), 0)
    turn = line >> 7
    to_y = y + jnp.where(turn == 0, 2, jnp.where(turn == 1, 1, jnp.where(turn == 2, 3, 0)))
    to_chip = (to_y & 3) * 16 + ((z + (line >> 5)) & 3) * 4 + ((x + (line >> 3)) & 3)
    sample = to_chip * 4 + ((line >> 2) & 1) * 2 + (line & 1)
    oneh[...] = (sample.astype(f32) == target).astype(f32).astype(bf16)

    def gather_grads(first, count):
        for p in range(first // 16, (first + count) // 16):
            n = 15 if p == 3 else 16
            slots = grecv.at[pl.ds(p * 16, n), pl.ds(0, WIN)]
            pltpu.make_async_copy(slots, slots, grsem.at[p]).wait()
        part = pl.ds(first * PITCH, count * PITCH)
        gh, gl = split(grecv[first : first + count].reshape(count * PITCH, 128))
        gg = jnp.concatenate([gh, gl], axis=1)

        def product(i):
            v = dot(oneh[i * 256 : i * 256 + 256, part], gg)
            return v[:, 0:128] + v[:, 128:256]

        return product

    ring_a2.finish()
    ring_b2.finish()
    product_a = gather_grads(0, 32)
    dense_a = [product_a(i) for i in range(2)]

    uh, ul = split(jnp.concatenate([ua[0, 0], ub[0, 0]], axis=0))
    u3 = jnp.concatenate([uh, ul, uh], axis=0)

    product_b = gather_grads(32, 32)
    upper = ((line[0:256] >> 1) & 1) == 0
    for i in range(2):
        dh, dl = split(dense_a[i] + product_b(i))
        both = dot(jnp.concatenate([dh, dh, dl], axis=1), u3)
        tiles = jnp.where(upper, both[:, 0:128], both[:, 128:256])
        sbuf[i * 32 : i * 32 + 32] = tiles.reshape(32, 8, 128)
        for p in (2 * i, 2 * i + 1):
            oy = TURNS[p]
            for oz, ox in PLANE:
                for kk in range(2):
                    if (oy, oz, ox) != (0, 0, 0):
                        remote(
                            sbuf.at[p * 16 + oz * 4 + ox, pl.ds(kk * 4, 4)],
                            srecv.at[k * 64 + chip, pl.ds(0, 4)],
                            sssem.at[0], srsem.at[0], (ys[oy], zs[oz], xs[ox], kk),
                        ).start()

    own = sbuf[48]
    srecv[k * 64 + chip, 0:4] = jnp.where(k == 0, own[0:4], own[4:8])
    other[0:4] = jnp.where(k == 0, own[4:8], own[0:4])
    last = remote(
        other.at[pl.ds(0, 4)], srecv.at[k * 64 + chip, pl.ds(0, 4)],
        xsend.at[0], xsend.at[1], partner,
    )
    last.start()
    done.append(last)

    slots = srecv.at[pl.ds(0, 126), pl.ds(0, 4)]
    pltpu.make_async_copy(slots, slots, srsem.at[0]).wait()
    last.wait_recv()
    tile = jnp.sum(srecv[:, 0:4], axis=0)
    d = chip * 2 + k
    for s in range(2):
        here = lax.broadcasted_iota(jnp.int32, (1, 256), 1) == 2 * d + s
        n = jnp.sum(jnp.where(here, len_ref[...], 0).astype(f32), axis=1, keepdims=True)
        for j in range(2):
            line = tile[j * 2 + s : j * 2 + s + 1] * score_scale
            out_ref[s : s + 1, j * 128 : j * 128 + 128] = line / n

    for cp in done:
        cp.wait_send()
    sent = gsend.at[pl.ds(0, 63), pl.ds(0, WIN)]
    pltpu.make_async_copy(sent, sent, gssem.at[0]).wait()
    sent = sbuf.at[pl.ds(0, 63)]
    pltpu.make_async_copy(sent, sent, sssem.at[0]).wait()


def body(hidden_in, out_grad, proj_in, proj_out, inverse_fisher, queries, lengths, offsets):
    vmem = pltpu.VMEM
    dma = pltpu.SemaphoreType.DMA
    anys = pl.BlockSpec(memory_space=pl.ANY)
    invm = pl.BlockSpec(memory_space=pltpu.VMEM)
    return pl.pallas_call(
        kernel,
        out_shape=pltpu.VMEM((2, 256), f32),
        in_specs=[anys] * 8,
        out_specs=invm,
        scratch_shapes=[
            vmem((16, 2, 128, 512), f32), vmem((512, 256), f32),
            vmem((7, 256, KCH), bf16), vmem((7, KCH, 128), bf16),
            vmem((2, 256, KCH), bf16), vmem((2, KCH, 128), bf16),
            vmem((1536, 256), bf16),
            vmem((2, 8, 2, 128, 256), f32), vmem((8, 2, 128, 256), f32),
            vmem((4, 4, 64, 256), f32), vmem((4, 4, 64, 256), f32),
            vmem((4, 64, 256), f32), vmem((4, 64, 256), f32),
            vmem((2, 4, 64, 256), f32), vmem((2, 4, 64, 256), f32),
            vmem((64, 256), f32), vmem((64, 256), f32),
            vmem((2, 64, 256), f32), vmem((2, 64, 256), f32),
            vmem((512, 128), f32), vmem((512, 128), f32), vmem((8, 16, 256), f32),
            vmem((64, PITCH, 128), f32), vmem((64, PITCH, 128), f32),
            vmem((512, 64 * PITCH), bf16),
            vmem((64, 8, 128), f32), vmem((128, 8, 128), f32), vmem((8, 128), f32),
            vmem((1, 256), jnp.int32), vmem((1, 256), jnp.int32),
            dma((16, 2)), dma((1,)), dma((2,)), dma((2, 7)), dma((2, 2)),
            dma((8,)), dma((8,)), dma((4, 10)), dma((4, 10)),
            pltpu.SemaphoreType.REGULAR, pltpu.SemaphoreType.REGULAR,
            dma((2,)), dma((2,)), dma((1,)), dma((4,)), dma((1,)), dma((1,)),
            dma((2,)),
        ],
        compiler_params=pltpu.CompilerParams(
            collective_id=0, has_side_effects=True, vmem_limit_bytes=60 * 1024 * 1024
        ),
    )(
        inverse_fisher, queries, hidden_in, proj_in, out_grad, proj_out,
        offsets.reshape(1, 256), lengths.reshape(1, 256),
    )


def solution(mesh):
    whole = Mesh(mesh.devices.reshape(4, 4, 4, 2), AXES)
    col = AXES[1:]
    return jax.shard_map(
        body,
        mesh=whole,
        in_specs=(
            P(AXES, None), P(AXES, None), P(), P(), P("row", col), P(col, None), P(), P(),
        ),
        out_specs=P(AXES, None),
        check_vma=False,
    )
```
